32 devices in a mesh: seq: 8 (over y, x, core), wt: 4 (over z).
Axes of the slice: x: 2, y: 2, z: 4, core: 2. Of those that a mesh axis runs over, the one named last changes fastest.
Arguments:
- layer_input: bfloat16 [1024, 2048], P(('seq', 'wt')), may hold values from -6 to 6
- token_shift_rates: float32 [5, 2048], replicated, may hold values from 0 to 1
- input_projection_weight: bfloat16 [3, 2048, 2048], P(None, None, 'wt'), may hold values from -0.125 to 0.125
- output_matrix: bfloat16 [2048, 2048], P('wt'), may hold values from -0.125 to 0.125
- decay_lowrank_first: bfloat16 [2048, 96], replicated, may hold values from -0.125 to 0.125
- decay_lowrank_second: bfloat16 [96, 2048], P(None, 'wt'), may hold values from -0.625 to 0.625
- learning_rate_first: bfloat16 [2048, 96], replicated, may hold values from -0.125 to 0.125
- learning_rate_second: bfloat16 [96, 2048], P(None, 'wt'), may hold values from -0.625 to 0.625
- decay_channel_bias: float32 [2048], P('wt'), may hold values from -10 to 1
- learning_rate_bias: float32 [2048], P('wt'), may hold values from -6 to 2
- prenorm_key_scale: float32 [2048], P('wt'), may hold values from 0.5 to 1.5
- written_key_share: float32 [2048], P('wt'), may hold values from 0 to 1
- present_step_coefficient: float32 [2048], P('wt'), may hold values from -3 to 3
- head_norm_gain: float32 [2048], P('wt'), may hold values from 0.5 to 1.5
- packed_request_length: int32 [8], replicated, may hold values from 1 to 512, 1024 in all
Outputs:
- layer_out: bfloat16 [1024, 2048], P(('seq', 'wt'))
The draws below stay inside these ranges and needn't reach their ends.
Inputs may be any that keep to these rules, and one draw needn't show every extreme that they name: `packed_request_length`: the 8 lengths sum to 1024, and the longest is exactly 512.
All inputs are finite; a program needn't handle non-finite values.
Results may differ from the reference program's by a relative error of at most 0.0069.
Values may be sent and summed in bfloat16 or wider, within the bound.
A program may use at most 128 MiB of HBM per device.

```python
import math
import jax
import jax.numpy as jnp
import numpy as np
from jax import lax

EMBED_DIMENSION = 2048
H = 32
HS = 64
RANK_W = 96
RANK_A = 96
REQS = 8
TOTAL_POSITIONS = 1024
MAXLEN = 512


def steps_of(rng, extent, split, low, top_value):
    level = 1.0
    for axis_at, parts in split:
        steps = jax.random.uniform(jax.random.fold_in(jax.random.fold_in(rng, 6), axis_at), (parts,), jnp.float32, low / len(split), top_value / len(split))
        level = level * jnp.repeat(jnp.exp(steps), extent[axis_at] // parts).reshape((-1,) + (1,) * (len(extent) - 1 - axis_at))
    return level


def length_profile(number_of, total, limit, slope):
    portions = [(1 << 20) // math.isqrt(grade ** slope) + 1 for grade in range(2, number_of + 1)]
    surplus, given = total - limit - (number_of - 1), [1] * (number_of - 1)
    while surplus > 0:
        movable = [i for i in range(number_of - 1) if given[i] < limit]
        mass, budget = sum([portions[i] for i in movable]), surplus
        for i in movable:
            more = min(limit - given[i], max(1, budget * portions[i] // mass), surplus)
            given[i] = given[i] + more
            surplus = surplus - more
    return np.array([limit] + given)


def ragged(key, amount, total, bound, slope):
    if amount == 2:
        one = jax.random.randint(key, (), max(1, total - bound), min(bound, total - 1) + 1)
        return jnp.stack([one, total - one])
    tallies = jnp.asarray(length_profile(amount, total, bound, slope), jnp.int32)
    pairs = (amount - 1) // 2
    giver, taker = tallies[1:1 + 2 * pairs:2], tallies[2:2 + 2 * pairs:2]
    room = jnp.minimum(giver - 1, bound - taker)
    moved = jax.random.randint(jax.random.fold_in(key, 1), (pairs,), 0, 1 << 20) % (room + 1)
    tallies = tallies.at[1:1 + 2 * pairs:2].set(giver - moved).at[2:2 + 2 * pairs:2].set(taker + moved)
    return tallies[jax.random.permutation(jax.random.fold_in(key, 2), amount)]


def normal_values(own_key, dims, width, most, pieces=(), kind=jnp.bfloat16):
    drawn = width * jax.random.normal(own_key, dims, jnp.float32)
    if pieces:
        drawn = drawn * steps_of(own_key, dims, pieces, -0.22, 0.18)
    return jnp.clip(drawn, -most, most).astype(kind)


def setup_inputs(seed: int = 0) -> dict:
    arg_keys = jax.random.split(jax.random.key(seed), 16)
    layer_input = normal_values(arg_keys[0], (TOTAL_POSITIONS, EMBED_DIMENSION), 1.0, 6.0, ((0, 32),))
    token_shift_rates = jnp.clip(jax.random.uniform(arg_keys[1], (5, EMBED_DIMENSION), jnp.float32, 0.0, 1.0), 0.0, 1.0)
    input_projection_weight = normal_values(arg_keys[2], (3, EMBED_DIMENSION, EMBED_DIMENSION), EMBED_DIMENSION ** -0.5, 0.125, ((2, 4),))
    output_matrix = normal_values(arg_keys[3], (EMBED_DIMENSION, EMBED_DIMENSION), EMBED_DIMENSION ** -0.5, 0.125, ((0, 4),))
    decay_lowrank_first = normal_values(arg_keys[4], (EMBED_DIMENSION, RANK_W), EMBED_DIMENSION ** -0.5, 0.125)
    decay_lowrank_second = normal_values(arg_keys[5], (RANK_W, EMBED_DIMENSION), RANK_W ** -0.5, 0.625, ((1, 4),))
    learning_rate_first = normal_values(arg_keys[6], (EMBED_DIMENSION, RANK_A), EMBED_DIMENSION ** -0.5, 0.125)
    learning_rate_second = normal_values(arg_keys[7], (RANK_A, EMBED_DIMENSION), RANK_A ** -0.5, 0.625, ((1, 4),))
    decay_channel_bias = jnp.clip(-10.0 + 11.0 * jax.random.uniform(arg_keys[8], (EMBED_DIMENSION,), jnp.float32) ** steps_of(arg_keys[8], (EMBED_DIMENSION,), ((0, 4),), -0.2, 0.2), -10.0, 1.0)
    learning_rate_bias = jnp.clip(-6.0 + 8.0 * jax.random.uniform(arg_keys[9], (EMBED_DIMENSION,), jnp.float32) ** steps_of(arg_keys[9], (EMBED_DIMENSION,), ((0, 4),), -0.2, 0.2), -6.0, 2.0)
    prenorm_key_scale = jnp.clip(0.5 + 1.0 * jax.random.uniform(arg_keys[10], (EMBED_DIMENSION,), jnp.float32) ** steps_of(arg_keys[10], (EMBED_DIMENSION,), ((0, 4),), -0.2, 0.2), 0.5, 1.5)
    written_key_share = jnp.clip(1.0 * jax.random.uniform(arg_keys[11], (EMBED_DIMENSION,), jnp.float32) ** steps_of(arg_keys[11], (EMBED_DIMENSION,), ((0, 4),), -0.2, 0.2), 0.0, 1.0)
    present_step_coefficient = normal_values(arg_keys[12], (EMBED_DIMENSION,), 0.5, 3.0, ((0, 4),), jnp.float32)
    head_norm_gain = jnp.clip(0.5 + 1.0 * jax.random.uniform(arg_keys[13], (EMBED_DIMENSION,), jnp.float32) ** steps_of(arg_keys[13], (EMBED_DIMENSION,), ((0, 4),), -0.2, 0.2), 0.5, 1.5)
    packed_request_length = ragged(arg_keys[14], REQS, TOTAL_POSITIONS, MAXLEN, 2).astype(jnp.int32)
    return {"layer_input": layer_input, "token_shift_rates": token_shift_rates, "input_projection_weight": input_projection_weight, "output_matrix": output_matrix, "decay_lowrank_first": decay_lowrank_first, "decay_lowrank_second": decay_lowrank_second, "learning_rate_first": learning_rate_first, "learning_rate_second": learning_rate_second, "decay_channel_bias": decay_channel_bias, "learning_rate_bias": learning_rate_bias, "prenorm_key_scale": prenorm_key_scale, "written_key_share": written_key_share, "present_step_coefficient": present_step_coefficient, "head_norm_gain": head_norm_gain, "packed_request_length": packed_request_length}


LOG_SCALE = 0.6065306597126334

def advance(memory, decay_row, unit_key, removal, values_t, keys_t):
    projected = lax.optimization_barrier(jnp.sum(memory * unit_key[..., None, :], axis=-1))
    kept = memory * decay_row[..., None, :] - projected[..., :, None] * removal[..., None, :]
    return kept + values_t[..., :, None] * keys_t[..., None, :]

def head_norm(heads_y, gain):
    center = heads_y - lax.optimization_barrier(jnp.mean(heads_y, axis=-1, keepdims=True))
    spread = lax.optimization_barrier(jnp.mean(center * center, axis=-1, keepdims=True))
    return center / jnp.sqrt(spread + 0.00064) * gain

def split_across_attention_groups(matrix):
    return matrix.reshape(matrix.shape[0], -1, HS)

def reference(layer_input, token_shift_rates, input_projection_weight, output_matrix, decay_lowrank_first, decay_lowrank_second, learning_rate_first, learning_rate_second, decay_channel_bias, learning_rate_bias, prenorm_key_scale, written_key_share, present_step_coefficient, head_norm_gain, packed_request_length):
    current = layer_input.astype(jnp.float32)
    starts = (jnp.cumsum(packed_request_length) - packed_request_length).astype(jnp.int32)
    positions = jnp.arange(TOTAL_POSITIONS, dtype=jnp.int32)
    resets = jnp.any(positions[:, None] == starts[None, :], axis=1)
    previous = jnp.concatenate([jnp.zeros((1, EMBED_DIMENSION), jnp.float32), current[:-1]], axis=0)
    previous = jnp.where(resets[:, None], jnp.zeros_like(previous), previous)
    mixed = [(current + (previous - current) * token_shift_rates[which]).astype(jnp.bfloat16) for which in range(5)]
    acceptance_vectors = jnp.dot(mixed[0], input_projection_weight[0], preferred_element_type=jnp.float32)
    keys = jnp.dot(mixed[1], input_projection_weight[1], preferred_element_type=jnp.float32)
    content_vectors = jnp.dot(mixed[2], input_projection_weight[2], preferred_element_type=jnp.float32)
    decay_low = jnp.tanh(jnp.dot(mixed[3], decay_lowrank_first, preferred_element_type=jnp.float32)).astype(jnp.bfloat16)
    decay = jnp.exp(-LOG_SCALE * jax.nn.sigmoid(decay_channel_bias + jnp.dot(decay_low, decay_lowrank_second, preferred_element_type=jnp.float32)))
    iclr_low = jnp.dot(mixed[4], learning_rate_first, preferred_element_type=jnp.float32).astype(jnp.bfloat16)
    rate = jax.nn.sigmoid(learning_rate_bias + jnp.dot(iclr_low, learning_rate_second, preferred_element_type=jnp.float32))
    scaled = split_across_attention_groups(keys * prenorm_key_scale)
    unit_key = scaled / jnp.sqrt(lax.optimization_barrier(jnp.sum(scaled * scaled, axis=-1, keepdims=True)) + 1e-06)
    removal = unit_key * split_across_attention_groups(rate)
    modified_lookup_vectors = keys * (1.0 + (rate - 1.0) * written_key_share)

    def step_token(memory, inputs):
        decay_t, unit_t, removal_t, value_t, key_t, recept_t, reset_t = inputs
        memory = jnp.where(reset_t, jnp.zeros_like(memory), memory)
        memory = advance(memory, decay_t, unit_t, removal_t, value_t, key_t)
        return (memory, lax.optimization_barrier(jnp.sum(memory * recept_t[:, None, :], axis=-1)))
    initial = jnp.zeros((H, HS, HS), jnp.float32)
    _, heads_y = lax.scan(step_token, initial, (split_across_attention_groups(decay), unit_key, removal, split_across_attention_groups(content_vectors), split_across_attention_groups(modified_lookup_vectors), split_across_attention_groups(acceptance_vectors), resets))
    rescaled_attention_groups = head_norm(heads_y, head_norm_gain.reshape(H, HS))
    diagonal_reward_contribution = lax.optimization_barrier(jnp.sum(split_across_attention_groups(acceptance_vectors * modified_lookup_vectors * present_step_coefficient), axis=-1, keepdims=True))
    combined_attention_groups = (rescaled_attention_groups + diagonal_reward_contribution * split_across_attention_groups(content_vectors)).reshape(TOTAL_POSITIONS, EMBED_DIMENSION).astype(jnp.bfloat16)
    return (current + jnp.dot(combined_attention_groups, output_matrix, preferred_element_type=jnp.float32)).astype(jnp.bfloat16)
```

```python
import functools
import jax
import jax.numpy as jnp
from jax import lax
from jax.experimental import pallas as pl
from jax.experimental.pallas import tpu as pltpu
from jax.sharding import PartitionSpec as P

HS = 64
LOG_SCALE = 0.6065306597126334
MESH = pl.DeviceIdType.MESH
F32 = jnp.float32
BF16 = jnp.bfloat16
STATE_TYPE = BF16


def mm(a, b, ca=1, cb=0):
    return lax.dot_general(
        a.astype(BF16), b.astype(BF16), (((ca,), (cb,)), ((), ())), preferred_element_type=F32
    )


def mm_full(a, b, ca=1, cb=0):
    return lax.dot_general(
        a, b, (((ca,), (cb,)), ((), ())), preferred_element_type=F32, precision=lax.Precision.HIGHEST
    )


def token_tables(first, rows, lengths):
    pos_c = first + lax.broadcasted_iota(jnp.int32, (rows, 1), 0)
    pos_r = first + lax.broadcasted_iota(jnp.int32, (1, rows), 1)
    far = jnp.int32(2**30)
    start = jnp.int32(0)
    reset = jnp.zeros((rows, 1), jnp.int32)
    seg_c = jnp.zeros((rows, 1), jnp.int32)
    seg_r = jnp.zeros((1, rows), jnp.int32)
    seg_last = jnp.int32(0)
    for length in lengths:
        reset = jnp.maximum(reset, jnp.where(pos_c == start, 1, 0))
        inside = jnp.where(start >= first, start, far)
        seg_c = seg_c + jnp.where(pos_c >= inside, 1, 0)
        seg_r = seg_r + jnp.where(pos_r >= inside, 1, 0)
        seg_last = seg_last + jnp.where(first + (rows - 1) >= inside, 1, 0)
        start = start + length
    return reset, seg_c, seg_r, seg_last


def head_slice(h):
    return slice(h * HS, (h + 1) * HS)


def per_head(fn, width):
    return jnp.concatenate([fn(head_slice(h)) for h in range(width // HS)], axis=1)


def block_terms(recept, keys, values, decay_in, rate_in, chan, seg_c, seg_r, seg_last):
    rows, width = keys.shape
    heads = width // HS
    decay_bias, rate_bias, key_scale, share = (chan[i : i + 1] for i in range(4))
    logw = -LOG_SCALE * jax.nn.sigmoid(decay_bias + decay_in)
    rate = jax.nn.sigmoid(rate_bias + rate_in)
    row = lax.broadcasted_iota(jnp.int32, (rows, rows), 0)
    col = lax.broadcasted_iota(jnp.int32, (rows, rows), 1)
    tri = jnp.where(row >= col, 1.0, 0.0).astype(F32)
    cum = mm_full(tri, logw)
    center = cum[rows // 2 - 1 : rows // 2]
    last = cum[rows - 1 : rows]
    grow = jnp.exp(cum - center)
    grow_x = jnp.exp(cum - logw - center)
    shrink = jnp.exp(center - cum)
    to_start = jnp.exp(center) * jnp.where(seg_c == 0, 1.0, 0.0)
    to_end = jnp.exp(last - center) * jnp.where(seg_c == seg_last, 1.0, 0.0)
    scaled = keys * key_scale
    squares = scaled * scaled
    norm = per_head(
        lambda s: jnp.broadcast_to(
            lax.rsqrt(jnp.sum(squares[:, s], axis=1, keepdims=True) + 1e-06), (rows, HS)
        ),
        width,
    )
    unit = scaled * norm
    keys_mod = keys * (1.0 + (rate - 1.0) * share)
    u_c = unit * grow_x
    q_c = recept * grow
    r_c = unit * rate * shrink
    k_c = keys_mod * shrink
    u_0 = u_c * to_start
    q_0 = q_c * to_start
    r_e = r_c * to_end
    k_e = k_c * to_end
    same = seg_c == seg_r
    strict = jnp.logical_and(same, row > col)
    causal = jnp.logical_and(same, row >= col)
    a_ur, a_uk, a_qr, a_qk = [], [], [], []
    for h in range(heads):
        s = head_slice(h)
        left = jnp.concatenate([u_c[:, s], q_c[:, s]], axis=0)
        right = jnp.concatenate([r_c[:, s], k_c[:, s]], axis=0)
        pair = mm(left, right, 1, 1)
        a_ur.append(jnp.where(strict, pair[:rows, :rows], 0.0))
        a_uk.append(jnp.where(strict, pair[:rows, rows:], 0.0).astype(BF16))
        a_qr.append(jnp.where(causal, pair[rows:, :rows], 0.0).astype(BF16))
        a_qk.append(jnp.where(causal, pair[rows:, rows:], 0.0).astype(BF16))
    eye = jnp.where(row == col, 1.0, 0.0)
    inverse = None
    size = 1
    while size < rows:
        tile_r, tile_c = row // size, col // size
        corner = jnp.logical_and(tile_r == tile_c + 1, tile_r % 2 == 1)
        lows = [jnp.where(corner, a, 0.0) for a in a_ur]
        if inverse is None:
            inverse = [eye - low for low in lows]
        else:
            halves = [mm(x, low) for x, low in zip(inverse, lows)]
            inverse = [x - mm(half, x) for x, half in zip(inverse, halves)]
        size *= 2
    small_r = lax.broadcasted_iota(jnp.int32, (HS, HS), 0)
    small_c = lax.broadcasted_iota(jnp.int32, (HS, HS), 1)
    decay_all = jnp.exp(last) * jnp.where(seg_last == 0, 1.0, 0.0)
    reads, offsets, maps, adds = [], [], [], []
    for h in range(heads):
        s = head_slice(h)
        v = values[:, s].astype(BF16)
        kv = mm(jnp.concatenate([a_uk[h], a_qk[h]], axis=0), v)
        solved = mm(inverse[h], jnp.concatenate([u_0[:, s], kv[:rows]], axis=1))
        out = jnp.concatenate([q_0[:, s], kv[rows:]], axis=1) - mm(a_qr[h], solved)
        reads.append(out[:, :HS])
        offsets.append(out[:, HS:])
        end = mm(r_e[:, s], solved, 0, 0)
        diag = jnp.where(small_r == small_c, jnp.broadcast_to(decay_all[:, s], (HS, HS)), 0.0)
        maps.append(diag - end[:, :HS])
        adds.append(mm(k_e[:, s], v, 0, 0) - end[:, HS:])
    return reads, offsets, maps, adds, keys_mod


def finish_heads(heads_y, recept, keys_mod, values, coefficient, gain):
    own = recept * keys_mod * coefficient
    mixed = []
    for h, y in enumerate(heads_y):
        s = head_slice(h)
        centered = y - jnp.mean(y, axis=1, keepdims=True)
        spread = jnp.mean(centered * centered, axis=1, keepdims=True)
        normed = centered * lax.rsqrt(spread + 0.00064) * gain[:, s]
        mixed.append(normed + jnp.sum(own[:, s], axis=1, keepdims=True) * values[:, s])
    return jnp.concatenate(mixed, axis=1).astype(BF16)


def kernel(
    n_seq, n_wt, hops,
    x_ref, rates_ref, win_hbm, wout_hbm, d1_ref, d2_ref, a1_ref, a2_ref, chan_ref, len_ref,
    out_ref,
    x_all, edge_src, edge_in, win, wout, lo_src, lo_in, part, part_16, rs_in,
    w_sem, edge_sem, fwd_sem, x_send, x_recv, lo_send, lo_recv, rs_send, rs_recv,
):
    b = lax.axis_index("seq")
    w = lax.axis_index("wt")
    shard, model = x_ref.shape
    rows = shard * n_wt
    width = win.shape[2]
    heads = width // HS
    piece = model // 8

    loads = [pltpu.make_async_copy(win_hbm.at[c], win.at[c], w_sem.at[c]) for c in range(3)]
    loads.append(pltpu.make_async_copy(wout_hbm, wout, w_sem.at[3]))
    for load in loads:
        load.start()

    def wt_peer(d):
        return (b, lax.rem(w + d, n_wt))

    def seq_peer(d):
        return (lax.rem(b + d, n_seq), w)

    barrier = pltpu.get_barrier_semaphore()
    for d in range(1, n_wt):
        pl.semaphore_signal(barrier, inc=1, device_id=wt_peer(d), device_id_type=MESH)
    for d in range(1, n_seq):
        pl.semaphore_signal(barrier, inc=1, device_id=seq_peer(d), device_id_type=MESH)
    last_row = x_ref[shard - 1 : shard, :].astype(F32)
    for i in range(8):
        edge_src[i : i + 1, :] = last_row[:, i * piece : (i + 1) * piece]
    mine = pl.ds(pl.multiple_of(w * shard, shard), shard)
    x_all[mine, :] = x_ref[...]
    pl.semaphore_wait(barrier, n_wt + n_seq - 2)

    def remote(src, dst, send, recv, target):
        return pltpu.make_async_remote_copy(
            src_ref=src, dst_ref=dst, send_sem=send, recv_sem=recv, device_id=target, device_id_type=MESH
        )

    edge_copy = remote(edge_src, edge_in, edge_sem.at[0], edge_sem.at[1], seq_peer(1))
    forwards = [
        remote(edge_in, edge_in, fwd_sem.at[d - 1], edge_sem.at[1], wt_peer(d)) for d in range(1, n_wt)
    ]
    is_last = w == n_wt - 1

    @pl.when(is_last)
    def _():
        edge_copy.start()

    x_copies = [
        remote(x_ref, x_all.at[mine], x_send.at[d - 1], x_recv.at[d - 1], wt_peer(d))
        for d in range(1, n_wt)
    ]
    for copy in x_copies:
        copy.start()
    edge_copy.wait_recv()

    @pl.when(is_last)
    def _():
        for copy in forwards:
            copy.start()
        edge_copy.wait_send()
        for copy in forwards:
            copy.wait_send()

    for copy in x_copies:
        copy.wait_recv()
    for load in loads[:3]:
        load.wait()

    lengths = [len_ref[i] for i in range(len_ref.shape[0])]
    reset, seg_c, seg_r, seg_last = token_tables(b * rows, rows, lengths)
    edge = jnp.concatenate([edge_in[i : i + 1, :] for i in range(8)], axis=1)
    first_row = lax.broadcasted_iota(jnp.int32, (rows, 1), 0) == 0
    sums = [None] * 5
    step = min(512, model)
    for k in range(0, model, step):
        cols = slice(k, k + step)
        current = x_all[:, cols].astype(F32)
        previous = jnp.where(first_row, edge[:, cols], pltpu.roll(current, 1, 0))
        previous = jnp.where(reset == 1, 0.0, previous)
        delta = previous - current
        for c in range(5):
            mixed = (current + delta * rates_ref[c : c + 1, cols]).astype(BF16)
            weight = (
                win[c, cols, :] if c < 3 else (d1_ref if c == 3 else a1_ref)[cols, :]
            )
            term = jnp.dot(mixed, weight, preferred_element_type=F32)
            sums[c] = term if sums[c] is None else sums[c] + term
    recept, keys, values = sums[:3]
    decay_in = jnp.dot(jnp.tanh(sums[3]).astype(BF16), d2_ref[...], preferred_element_type=F32)
    rate_in = jnp.dot(sums[4].astype(BF16), a2_ref[...], preferred_element_type=F32)
    chan = chan_ref[...]
    reads, offsets, maps, adds, keys_mod = block_terms(
        recept, keys, values, decay_in, rate_in, chan, seg_c, seg_r, seg_last
    )
    for h in range(heads):
        lo_src[0, :, head_slice(h)] = maps[h].astype(STATE_TYPE)
        lo_src[1, :, head_slice(h)] = adds[h].astype(STATE_TYPE)
    lo_copies = [
        remote(lo_src, lo_in.at[d - 1], lo_send.at[d - 1], lo_recv.at[d - 1], seq_peer(d))
        for d in range(1, hops)
    ]
    lo_copies.append(
        remote(
            lo_src.at[1], lo_in.at[hops - 1, 1], lo_send.at[hops - 1], lo_recv.at[hops - 1], seq_peer(hops)
        )
    )
    for copy in lo_copies:
        copy.start()
    for copy in lo_copies:
        copy.wait_recv()
    state = [lo_in[hops - 1, 1, :, head_slice(h)].astype(F32) for h in range(heads)]
    for d in range(hops - 2, -1, -1):
        state = [
            mm(lo_in[d, 0, :, head_slice(h)], state[h]) + lo_in[d, 1, :, head_slice(h)].astype(F32)
            for h in range(heads)
        ]
    heads_y = [mm(reads[h], state[h]) + offsets[h] for h in range(heads)]
    head_mix = finish_heads(heads_y, recept, keys_mod, values, chan[4:5], chan[5:6])

    loads[3].wait()
    for k in range(0, model, step):
        cols = slice(k, k + step)
        term = jnp.dot(head_mix, wout[:, cols], preferred_element_type=F32)
        part[:, cols] = term
        part_16[:, cols] = term.astype(BF16)
    rs_copies = []
    for d in range(1, n_wt):
        there = pl.ds(pl.multiple_of(lax.rem(w + d, n_wt) * shard, shard), shard)
        rs_copies.append(
            remote(part_16.at[there], rs_in.at[d - 1], rs_send.at[d - 1], rs_recv.at[d - 1], wt_peer(d))
        )
    for copy in rs_copies:
        copy.start()
    total = part[mine, :] + x_ref[...].astype(F32)
    for d, copy in enumerate(rs_copies):
        copy.wait_recv()
        total = total + rs_in[d].astype(F32)
    out_ref[...] = total.astype(out_ref.dtype)
    for copy in x_copies + lo_copies + rs_copies:
        copy.wait_send()


def shards(
    n_seq, n_wt,
    layer_input, token_shift_rates, input_projection_weight, output_matrix,
    decay_lowrank_first, decay_lowrank_second, learning_rate_first, learning_rate_second,
    decay_channel_bias, learning_rate_bias, prenorm_key_scale, written_key_share,
    present_step_coefficient, head_norm_gain, packed_request_length,
):
    shard, model = layer_input.shape
    rows = shard * n_wt
    width = decay_lowrank_second.shape[1]
    hops = (n_seq + 1) // 2
    chan = jnp.stack(
        [
            decay_channel_bias, learning_rate_bias, prenorm_key_scale,
            written_key_share, present_step_coefficient, head_norm_gain,
        ]
    )
    vmem = pl.BlockSpec(memory_space=pltpu.VMEM)
    far = pl.BlockSpec(memory_space=pl.ANY)
    dma = pltpu.SemaphoreType.DMA
    return pl.pallas_call(
        functools.partial(kernel, n_seq, n_wt, hops),
        out_shape=jax.ShapeDtypeStruct((shard, model), BF16),
        in_specs=[vmem, vmem, far, far, vmem, vmem, vmem, vmem, vmem, pl.BlockSpec(memory_space=pltpu.SMEM)],
        out_specs=vmem,
        scratch_shapes=[
            pltpu.VMEM((rows, model), BF16),
            pltpu.VMEM((8, model // 8), F32),
            pltpu.VMEM((8, model // 8), F32),
            pltpu.VMEM((3, model, width), BF16),
            pltpu.VMEM((width, model), BF16),
            pltpu.VMEM((2, HS, width), STATE_TYPE),
            pltpu.VMEM((hops, 2, HS, width), STATE_TYPE),
            pltpu.VMEM((rows, model), F32),
            pltpu.VMEM((rows, model), BF16),
            pltpu.VMEM((n_wt - 1, shard, model), BF16),
            dma((4,)), dma((2,)), dma((n_wt - 1,)),
            dma((n_wt - 1,)), dma((n_wt - 1,)),
            dma((hops,)), dma((hops,)),
            dma((n_wt - 1,)), dma((n_wt - 1,)),
        ],
        compiler_params=pltpu.CompilerParams(
            collective_id=0, has_side_effects=True, vmem_limit_bytes=56 * 1024 * 1024
        ),
    )(
        layer_input, token_shift_rates, input_projection_weight, output_matrix,
        decay_lowrank_first, decay_lowrank_second, learning_rate_first, learning_rate_second,
        chan, packed_request_length,
    )


def solution(mesh):
    placed = (
        P(("seq", "wt"), None),
        P(),
        P(None, None, "wt"),
        P("wt", None),
        P(),
        P(None, "wt"),
        P(),
        P(None, "wt"),
        P("wt"),
        P("wt"),
        P("wt"),
        P("wt"),
        P("wt"),
        P("wt"),
        P(),
    )
    return jax.shard_map(
        functools.partial(shards, mesh.shape["seq"], mesh.shape["wt"]),
        mesh=mesh, in_specs=placed, out_specs=P(("seq", "wt"), None), check_vma=False,
    )
```

```python
import functools
import jax
import jax.numpy as jnp
from jax import lax
from jax.experimental import pallas as pl
from jax.experimental.pallas import tpu as pltpu
from jax.sharding import PartitionSpec as P

HS = 64
LOG_SCALE = 0.6065306597126334
MESH = pl.DeviceIdType.MESH
F32 = jnp.float32
BF16 = jnp.bfloat16
STATE_TYPE = BF16


def mm(a, b, ca=1, cb=0):
    return lax.dot_general(
        a.astype(BF16), b.astype(BF16), (((ca,), (cb,)), ((), ())), preferred_element_type=F32
    )


def mm_full(a, b, ca=1, cb=0):
    return lax.dot_general(
        a, b, (((ca,), (cb,)), ((), ())), preferred_element_type=F32, precision=lax.Precision.HIGHEST
    )


def token_tables(first, rows, lengths):
    pos_c = first + lax.broadcasted_iota(jnp.int32, (rows, 1), 0)
    pos_r = first + lax.broadcasted_iota(jnp.int32, (1, rows), 1)
    far = jnp.int32(2**30)
    start = jnp.int32(0)
    reset = jnp.zeros((rows, 1), jnp.int32)
    seg_c = jnp.zeros((rows, 1), jnp.int32)
    seg_r = jnp.zeros((1, rows), jnp.int32)
    seg_last = jnp.int32(0)
    for length in lengths:
        reset = jnp.maximum(reset, jnp.where(pos_c == start, 1, 0))
        inside = jnp.where(start >= first, start, far)
        seg_c = seg_c + jnp.where(pos_c >= inside, 1, 0)
        seg_r = seg_r + jnp.where(pos_r >= inside, 1, 0)
        seg_last = seg_last + jnp.where(first + (rows - 1) >= inside, 1, 0)
        start = start + length
    return reset, seg_c, seg_r, seg_last


def head_slice(h):
    return slice(h * HS, (h + 1) * HS)


def per_head(fn, width):
    return jnp.concatenate([fn(head_slice(h)) for h in range(width // HS)], axis=1)


def block_terms(recept, keys, values, decay_in, rate_in, chan, seg_c, seg_r, seg_last):
    rows, width = keys.shape
    heads = width // HS
    decay_bias, rate_bias, key_scale, share = chan[:4]
    logw = -LOG_SCALE * jax.nn.sigmoid(decay_bias + decay_in)
    rate = jax.nn.sigmoid(rate_bias + rate_in)
    row = lax.broadcasted_iota(jnp.int32, (rows, rows), 0)
    col = lax.broadcasted_iota(jnp.int32, (rows, rows), 1)
    tri = jnp.where(row >= col, 1.0, 0.0).astype(F32)
    cum = mm_full(tri, logw)
    center = cum[rows // 2 - 1 : rows // 2]
    last = cum[rows - 1 : rows]
    grow = jnp.exp(cum - center)
    grow_x = jnp.exp(cum - logw - center)
    shrink = jnp.exp(center - cum)
    to_start = jnp.exp(center) * jnp.where(seg_c == 0, 1.0, 0.0)
    to_end = jnp.exp(last - center) * jnp.where(seg_c == seg_last, 1.0, 0.0)
    scaled = keys * key_scale
    squares = scaled * scaled
    norm = per_head(
        lambda s: jnp.broadcast_to(
            lax.rsqrt(jnp.sum(squares[:, s], axis=1, keepdims=True) + 1e-06), (rows, HS)
        ),
        width,
    )
    unit = scaled * norm
    keys_mod = keys * (1.0 + (rate - 1.0) * share)
    u_c = unit * grow_x
    q_c = recept * grow
    r_c = unit * rate * shrink
    k_c = keys_mod * shrink
    u_0 = u_c * to_start
    q_0 = q_c * to_start
    r_e = r_c * to_end
    k_e = k_c * to_end
    same = seg_c == seg_r
    strict = jnp.logical_and(same, row > col)
    causal = jnp.logical_and(same, row >= col)
    a_ur, a_uk, a_qr, a_qk = [], [], [], []
    for h in range(heads):
        s = head_slice(h)
        left = jnp.concatenate([u_c[:, s], q_c[:, s]], axis=0)
        right = jnp.concatenate([r_c[:, s], k_c[:, s]], axis=0)
        pair = mm(left, right, 1, 1)
        a_ur.append(jnp.where(strict, pair[:rows, :rows], 0.0))
        a_uk.append(jnp.where(strict, pair[:rows, rows:], 0.0).astype(BF16))
        a_qr.append(jnp.where(causal, pair[rows:, :rows], 0.0).astype(BF16))
        a_qk.append(jnp.where(causal, pair[rows:, rows:], 0.0).astype(BF16))
    eye = jnp.where(row == col, 1.0, 0.0)
    inverse = None
    size = 1
    while size < rows:
        tile_r, tile_c = row // size, col // size
        corner = jnp.logical_and(tile_r == tile_c + 1, tile_r % 2 == 1)
        lows = [jnp.where(corner, a, 0.0) for a in a_ur]
        if inverse is None:
            inverse = [eye - low for low in lows]
        else:
            halves = [mm(x, low) for x, low in zip(inverse, lows)]
            inverse = [x - mm(half, x) for x, half in zip(inverse, halves)]
        size *= 2
    small_r = lax.broadcasted_iota(jnp.int32, (HS, HS), 0)
    small_c = lax.broadcasted_iota(jnp.int32, (HS, HS), 1)
    decay_all = jnp.exp(last) * jnp.where(seg_last == 0, 1.0, 0.0)
    maps, adds, pending = [], [], []
    for h in range(heads):
        s = head_slice(h)
        v = values[:, s].astype(BF16)
        kv = mm(jnp.concatenate([a_uk[h], a_qk[h]], axis=0), v)
        solved = mm(inverse[h], jnp.concatenate([u_0[:, s], kv[:rows]], axis=1)).astype(BF16)
        end = mm(r_e[:, s], solved, 0, 0)
        diag = jnp.where(small_r == small_c, jnp.broadcast_to(decay_all[:, s], (HS, HS)), 0.0)
        maps.append(diag - end[:, :HS])
        adds.append(mm(k_e[:, s], v, 0, 0) - end[:, HS:])
        pending.append((a_qr[h], solved, q_0[:, s], kv[rows:]))
    return maps, adds, pending, keys_mod


def read_terms(pending):
    reads, offsets = [], []
    for a_qr, solved, q_0, direct in pending:
        out = jnp.concatenate([q_0, direct], axis=1) - mm(a_qr, solved)
        reads.append(out[:, :HS].astype(BF16))
        offsets.append(out[:, HS:])
    return reads, offsets


def finish_heads(heads_y, recept, keys_mod, values, coefficient, gain):
    own = recept * keys_mod * coefficient
    mixed = []
    for h, y in enumerate(heads_y):
        s = head_slice(h)
        centered = y - jnp.mean(y, axis=1, keepdims=True)
        spread = jnp.mean(centered * centered, axis=1, keepdims=True)
        normed = centered * lax.rsqrt(spread + 0.00064) * gain[:, s]
        mixed.append(normed + jnp.sum(own[:, s], axis=1, keepdims=True) * values[:, s])
    return jnp.concatenate(mixed, axis=1).astype(BF16)


def kernel(
    n_seq, n_wt, hops,
    x_ref, rates_ref, win_hbm, wout_hbm, d1_ref, d2_ref, a1_ref, a2_ref,
    db_ref, rb_ref, ks_ref, sh_ref, co_ref, ga_ref, len_ref,
    out_ref,
    x_all, edge_src, edge_in, win, wout, lo_src, lo_in, part, part_16, rs_in, pair_in, chip_src,
    w_sem, pair_sem, edge_sem, fwd_sem, x_send, x_recv, lo_send, lo_recv, rs_send, rs_recv,
):
    b = lax.axis_index("seq")
    w = lax.axis_index("wt")
    shard, model = x_ref.shape
    rows = shard * n_wt
    width = win.shape[2]
    heads = width // HS
    odd = lax.rem(b, 2)
    piece = model // 8

    loads = [pltpu.make_async_copy(win_hbm.at[c], win.at[c], w_sem.at[c]) for c in range(3)]
    loads.append(pltpu.make_async_copy(wout_hbm, wout, w_sem.at[3]))
    for load in loads:
        load.start()

    def wt_peer(d):
        return (b, lax.rem(w + d, n_wt))

    def seq_peer(d):
        return (lax.rem(b + d, n_seq), w)

    barrier = pltpu.get_barrier_semaphore()
    for d in range(1, n_wt):
        pl.semaphore_signal(barrier, inc=1, device_id=wt_peer(d), device_id_type=MESH)
    for d in range(1, n_seq):
        pl.semaphore_signal(barrier, inc=1, device_id=seq_peer(d), device_id_type=MESH)
    last_row = x_ref[shard - 1 : shard, :].astype(F32)
    for i in range(8):
        edge_src[i : i + 1, :] = last_row[:, i * piece : (i + 1) * piece]
    mine = pl.ds(pl.multiple_of(w * shard, shard), shard)
    x_all[mine, :] = x_ref[...]
    pl.semaphore_wait(barrier, n_wt + n_seq - 2)

    def remote(src, dst, send, recv, target):
        return pltpu.make_async_remote_copy(
            src_ref=src, dst_ref=dst, send_sem=send, recv_sem=recv, device_id=target, device_id_type=MESH
        )

    edge_copy = remote(edge_src, edge_in, edge_sem.at[0], edge_sem.at[1], seq_peer(1))
    forwards = [
        remote(edge_in, edge_in, fwd_sem.at[d - 1], edge_sem.at[1], wt_peer(d)) for d in range(1, n_wt)
    ]
    is_last = w == n_wt - 1

    @pl.when(is_last)
    def _():
        edge_copy.start()

    x_copies = [
        remote(x_ref, x_all.at[mine], x_send.at[d - 1], x_recv.at[d - 1], wt_peer(d))
        for d in range(1, n_wt)
    ]
    for copy in x_copies:
        copy.start()
    edge_copy.wait_recv()

    @pl.when(is_last)
    def _():
        for copy in forwards:
            copy.start()
        edge_copy.wait_send()
        for copy in forwards:
            copy.wait_send()

    for copy in x_copies:
        copy.wait_recv()
    for load in loads[:3]:
        load.wait()

    lengths = [len_ref[i] for i in range(len_ref.shape[0])]
    reset, seg_c, seg_r, seg_last = token_tables(b * rows, rows, lengths)
    edge = jnp.concatenate([edge_in[i : i + 1, :] for i in range(8)], axis=1)
    first_row = lax.broadcasted_iota(jnp.int32, (rows, 1), 0) == 0
    sums = [None] * 5
    step = min(512, model)
    for k in range(0, model, step):
        cols = slice(k, k + step)
        current = x_all[:, cols].astype(F32)
        previous = jnp.where(first_row, edge[:, cols], pltpu.roll(current, 1, 0))
        previous = jnp.where(reset == 1, 0.0, previous)
        delta = previous - current
        for c in range(5):
            mixed = (current + delta * rates_ref[c : c + 1, cols]).astype(BF16)
            if c < 3:
                term = mm(mixed, win[c, cols, :])
            else:
                term = mm(mixed, (d1_ref if c == 3 else a1_ref)[:, cols], 1, 1)
            sums[c] = term if sums[c] is None else sums[c] + term
    recept, keys, values = sums[:3]
    decay_in = jnp.dot(jnp.tanh(sums[3]).astype(BF16), d2_ref[...], preferred_element_type=F32)
    rate_in = jnp.dot(sums[4].astype(BF16), a2_ref[...], preferred_element_type=F32)
    chan = [ref[...] for ref in (db_ref, rb_ref, ks_ref, sh_ref, co_ref, ga_ref)]
    maps, adds, pending, keys_mod = block_terms(
        recept, keys, values, decay_in, rate_in, chan, seg_c, seg_r, seg_last
    )
    for h in range(heads):
        lo_src[0, :, head_slice(h)] = maps[h].astype(STATE_TYPE)
        lo_src[1, :, head_slice(h)] = adds[h].astype(STATE_TYPE)
    pair_copy = remote(lo_src, pair_in, pair_sem.at[0], pair_sem.at[1], (b + 1 - 2 * odd, w))
    pair_copy.start()
    reads, offsets = read_terms(pending)
    pair_copy.wait_recv()
    is_odd = odd == 1
    mine_lo = lo_src[...].astype(F32)
    other_lo = pair_in[...].astype(F32)
    even_lo = jnp.where(is_odd, other_lo, mine_lo)
    odd_lo = jnp.where(is_odd, mine_lo, other_lo)
    for h in range(heads):
        s = head_slice(h)
        both = mm(odd_lo[0, :, s], jnp.concatenate([even_lo[0, :, s], even_lo[1, :, s]], axis=1))
        chip_src[0, :, s] = both[:, :HS].astype(STATE_TYPE)
        chip_src[1, :, s] = (both[:, HS:] + odd_lo[1, :, s]).astype(STATE_TYPE)
    lo_copies = [
        remote(chip_src, lo_in.at[d - 1], lo_send.at[d - 1], lo_recv.at[d - 1], seq_peer(2 * d))
        for d in range(1, hops)
    ]
    lo_copies.append(
        remote(
            chip_src.at[1], lo_in.at[hops - 1, 1], lo_send.at[hops - 1], lo_recv.at[hops - 1],
            seq_peer(2 * hops),
        )
    )
    for copy in lo_copies:
        copy.start()
    for copy in lo_copies:
        copy.wait_recv()
    lo_copies.append(pair_copy)
    state = [lo_in[hops - 1, 1, :, head_slice(h)].astype(F32) for h in range(heads)]
    for d in range(hops - 2, -1, -1):
        state = [
            mm(lo_in[d, 0, :, head_slice(h)], state[h]) + lo_in[d, 1, :, head_slice(h)].astype(F32)
            for h in range(heads)
        ]
    state = [
        jnp.where(
            is_odd,
            mm(even_lo[0, :, head_slice(h)], state[h]) + even_lo[1, :, head_slice(h)],
            state[h],
        )
        for h in range(heads)
    ]
    heads_y = [mm(reads[h], state[h]) + offsets[h] for h in range(heads)]
    head_mix = finish_heads(heads_y, recept, keys_mod, values, chan[4], chan[5])

    loads[3].wait()
    for k in range(0, model, step):
        cols = slice(k, k + step)
        term = jnp.dot(head_mix, wout[:, cols], preferred_element_type=F32)
        part[:, cols] = term
        part_16[:, cols] = term.astype(BF16)
    rs_copies = []
    for d in range(1, n_wt):
        there = pl.ds(pl.multiple_of(lax.rem(w + d, n_wt) * shard, shard), shard)
        rs_copies.append(
            remote(part_16.at[there], rs_in.at[d - 1], rs_send.at[d - 1], rs_recv.at[d - 1], wt_peer(d))
        )
    for copy in rs_copies:
        copy.start()
    total = part[mine, :] + x_ref[...].astype(F32)
    for d, copy in enumerate(rs_copies):
        copy.wait_recv()
        total = total + rs_in[d].astype(F32)
    out_ref[...] = total.astype(out_ref.dtype)
    for copy in x_copies + lo_copies + rs_copies:
        copy.wait_send()


def shards(
    n_seq, n_wt,
    layer_input, token_shift_rates, input_projection_weight, output_matrix,
    decay_lowrank_first, decay_lowrank_second, learning_rate_first, learning_rate_second,
    decay_channel_bias, learning_rate_bias, prenorm_key_scale, written_key_share,
    present_step_coefficient, head_norm_gain, packed_request_length,
):
    shard, model = layer_input.shape
    rows = shard * n_wt
    width = decay_lowrank_second.shape[1]
    hops = (n_seq // 2 + 1) // 2
    chan = [
        v.reshape(1, width)
        for v in (
            decay_channel_bias, learning_rate_bias, prenorm_key_scale,
            written_key_share, present_step_coefficient, head_norm_gain,
        )
    ]
    vmem = pl.BlockSpec(memory_space=pltpu.VMEM)
    far = pl.BlockSpec(memory_space=pl.ANY)
    dma = pltpu.SemaphoreType.DMA
    return pl.pallas_call(
        functools.partial(kernel, n_seq, n_wt, hops),
        out_shape=jax.ShapeDtypeStruct((shard, model), BF16),
        in_specs=[vmem, vmem, far, far] + [vmem] * 10 + [pl.BlockSpec(memory_space=pltpu.SMEM)],
        out_specs=vmem,
        scratch_shapes=[
            pltpu.VMEM((rows, model), BF16),
            pltpu.VMEM((8, model // 8), F32),
            pltpu.VMEM((8, model // 8), F32),
            pltpu.VMEM((3, model, width), BF16),
            pltpu.VMEM((width, model), BF16),
            pltpu.VMEM((2, HS, width), STATE_TYPE),
            pltpu.VMEM((hops, 2, HS, width), STATE_TYPE),
            pltpu.VMEM((rows, model), F32),
            pltpu.VMEM((rows, model), BF16),
            pltpu.VMEM((n_wt - 1, shard, model), BF16),
            pltpu.VMEM((2, HS, width), STATE_TYPE),
            pltpu.VMEM((2, HS, width), STATE_TYPE),
            dma((4,)), dma((2,)), dma((2,)), dma((n_wt - 1,)),
            dma((n_wt - 1,)), dma((n_wt - 1,)),
            dma((hops,)), dma((hops,)),
            dma((n_wt - 1,)), dma((n_wt - 1,)),
        ],
        compiler_params=pltpu.CompilerParams(
            collective_id=0, has_side_effects=True, vmem_limit_bytes=56 * 1024 * 1024
        ),
    )(
        layer_input, token_shift_rates, input_projection_weight, output_matrix,
        decay_lowrank_first.T, decay_lowrank_second, learning_rate_first.T, learning_rate_second,
        *chan, packed_request_length,
    )


def solution(mesh):
    placed = (
        P(("seq", "wt"), None),
        P(),
        P(None, None, "wt"),
        P("wt", None),
        P(),
        P(None, "wt"),
        P(),
        P(None, "wt"),
        P("wt"),
        P("wt"),
        P("wt"),
        P("wt"),
        P("wt"),
        P("wt"),
        P(),
    )
    return jax.shard_map(
        functools.partial(shards, mesh.shape["seq"], mesh.shape["wt"]),
        mesh=mesh, in_specs=placed, out_specs=P(("seq", "wt"), None), check_vma=False,
    )
```

```python
import functools
import jax
import jax.numpy as jnp
from jax import lax
from jax.experimental import pallas as pl
from jax.experimental.pallas import tpu as pltpu
from jax.sharding import PartitionSpec as P

HS = 64
LOG_SCALE = 0.6065306597126334
MESH = pl.DeviceIdType.MESH
F32 = jnp.float32
BF16 = jnp.bfloat16
STATE_TYPE = BF16


def mm(a, b, ca=1, cb=0):
    return lax.dot_general(
        a.astype(BF16), b.astype(BF16), (((ca,), (cb,)), ((), ())), preferred_element_type=F32
    )


def mm_full(a, b, ca=1, cb=0):
    return lax.dot_general(
        a, b, (((ca,), (cb,)), ((), ())), preferred_element_type=F32, precision=lax.Precision.HIGHEST
    )


def token_tables(first, rows, lengths):
    pos_c = first + lax.broadcasted_iota(jnp.int32, (rows, 1), 0)
    pos_r = first + lax.broadcasted_iota(jnp.int32, (1, rows), 1)
    far = jnp.int32(2**30)
    start = jnp.int32(0)
    reset = jnp.zeros((rows, 1), jnp.int32)
    seg_c = jnp.zeros((rows, 1), jnp.int32)
    seg_r = jnp.zeros((1, rows), jnp.int32)
    seg_last = jnp.int32(0)
    for length in lengths:
        reset = jnp.maximum(reset, jnp.where(pos_c == start, 1, 0))
        inside = jnp.where(start >= first, start, far)
        seg_c = seg_c + jnp.where(pos_c >= inside, 1, 0)
        seg_r = seg_r + jnp.where(pos_r >= inside, 1, 0)
        seg_last = seg_last + jnp.where(first + (rows - 1) >= inside, 1, 0)
        start = start + length
    return reset, seg_c, seg_r, seg_last


def head_slice(h):
    return slice(h * HS, (h + 1) * HS)


def per_head(fn, width):
    return jnp.concatenate([fn(head_slice(h)) for h in range(width // HS)], axis=1)


def block_terms(recept, keys, values, decay_in, rate_in, chan, seg_c, seg_r, seg_last):
    rows, width = keys.shape
    heads = width // HS
    decay_bias, rate_bias, key_scale, share = chan[:4]
    logw = -LOG_SCALE * jax.nn.sigmoid(decay_bias + decay_in)
    rate = jax.nn.sigmoid(rate_bias + rate_in)
    row = lax.broadcasted_iota(jnp.int32, (rows, rows), 0)
    col = lax.broadcasted_iota(jnp.int32, (rows, rows), 1)
    tri = jnp.where(row >= col, 1.0, 0.0).astype(F32)
    cum = mm_full(tri, logw)
    center = cum[rows // 2 - 1 : rows // 2]
    last = cum[rows - 1 : rows]
    grow = jnp.exp(cum - center)
    grow_x = jnp.exp(cum - logw - center)
    shrink = jnp.exp(center - cum)
    to_start = jnp.exp(center) * jnp.where(seg_c == 0, 1.0, 0.0)
    to_end = jnp.exp(last - center) * jnp.where(seg_c == seg_last, 1.0, 0.0)
    scaled = keys * key_scale
    squares = scaled * scaled
    norm = per_head(
        lambda s: jnp.broadcast_to(
            lax.rsqrt(jnp.sum(squares[:, s], axis=1, keepdims=True) + 1e-06), (rows, HS)
        ),
        width,
    )
    unit = scaled * norm
    keys_mod = keys * (1.0 + (rate - 1.0) * share)
    u_c = unit * grow_x
    q_c = recept * grow
    r_c = unit * rate * shrink
    k_c = keys_mod * shrink
    u_0 = u_c * to_start
    q_0 = q_c * to_start
    r_e = r_c * to_end
    k_e = k_c * to_end
    same = seg_c == seg_r
    strict = jnp.logical_and(same, row > col)
    causal = jnp.logical_and(same, row >= col)
    a_ur, a_uk, a_qr, a_qk = [], [], [], []
    for h in range(heads):
        s = head_slice(h)
        left = jnp.concatenate([u_c[:, s], q_c[:, s]], axis=0)
        right = jnp.concatenate([r_c[:, s], k_c[:, s]], axis=0)
        pair = mm(left, right, 1, 1)
        a_ur.append(jnp.where(strict, pair[:rows, :rows], 0.0))
        a_uk.append(jnp.where(strict, pair[:rows, rows:], 0.0).astype(BF16))
        a_qr.append(jnp.where(causal, pair[rows:, :rows], 0.0).astype(BF16))
        a_qk.append(jnp.where(causal, pair[rows:, rows:], 0.0).astype(BF16))
    eye = jnp.where(row == col, 1.0, 0.0)
    inverse = None
    size = 1
    while size < rows:
        tile_r, tile_c = row // size, col // size
        corner = jnp.logical_and(tile_r == tile_c + 1, tile_r % 2 == 1)
        lows = [jnp.where(corner, a, 0.0) for a in a_ur]
        if inverse is None:
            inverse = [eye - low for low in lows]
        else:
            halves = [mm(x, low) for x, low in zip(inverse, lows)]
            inverse = [x - mm(half, x) for x, half in zip(inverse, halves)]
        size *= 2
    small_r = lax.broadcasted_iota(jnp.int32, (HS, HS), 0)
    small_c = lax.broadcasted_iota(jnp.int32, (HS, HS), 1)
    decay_all = jnp.exp(last) * jnp.where(seg_last == 0, 1.0, 0.0)
    maps, adds, pending = [], [], []
    for h in range(heads):
        s = head_slice(h)
        v = values[:, s].astype(BF16)
        kv = mm(jnp.concatenate([a_uk[h], a_qk[h]], axis=0), v)
        solved = mm(inverse[h], jnp.concatenate([u_0[:, s], kv[:rows]], axis=1)).astype(BF16)
        end = mm(r_e[:, s], solved, 0, 0)
        diag = jnp.where(small_r == small_c, jnp.broadcast_to(decay_all[:, s], (HS, HS)), 0.0)
        maps.append(diag - end[:, :HS])
        adds.append(mm(k_e[:, s], v, 0, 0) - end[:, HS:])
        pending.append((a_qr[h], solved, q_0[:, s], kv[rows:]))
    return maps, adds, pending, keys_mod


def read_terms(pending):
    reads, offsets = [], []
    for a_qr, solved, q_0, direct in pending:
        out = jnp.concatenate([q_0, direct], axis=1) - mm(a_qr, solved)
        reads.append(out[:, :HS].astype(BF16))
        offsets.append(out[:, HS:])
    return reads, offsets


def finish_heads(heads_y, recept, keys_mod, values, coefficient, gain):
    own = recept * keys_mod * coefficient
    mixed = []
    for h, y in enumerate(heads_y):
        s = head_slice(h)
        centered = y - jnp.mean(y, axis=1, keepdims=True)
        spread = jnp.mean(centered * centered, axis=1, keepdims=True)
        normed = centered * lax.rsqrt(spread + 0.00064) * gain[:, s]
        mixed.append(normed + jnp.sum(own[:, s], axis=1, keepdims=True) * values[:, s])
    return jnp.concatenate(mixed, axis=1).astype(BF16)


def kernel(
    n_seq, n_wt, hops,
    x_ref, rates_ref, win_hbm, wout_hbm, d1_ref, d2_ref, a1_ref, a2_ref,
    db_ref, rb_ref, ks_ref, sh_ref, co_ref, ga_ref, len_ref,
    out_ref,
    x_all, edge_src, edge_in, win, wout, lo_src, lo_in, part, acc, rs_src, rs_in, pair_in, chip_src,
    w_sem, pair_sem, edge_sem, fwd_sem, x_send, x_recv, lo_send, lo_recv, rs_send, rs_recv,
):
    b = lax.axis_index("seq")
    w = lax.axis_index("wt")
    shard, model = x_ref.shape
    rows = shard * n_wt
    width = win.shape[2]
    heads = width // HS
    odd = lax.rem(b, 2)
    piece = model // 8

    loads = [pltpu.make_async_copy(win_hbm.at[c], win.at[c], w_sem.at[c]) for c in range(3)]
    loads.append(pltpu.make_async_copy(wout_hbm, wout, w_sem.at[3]))
    for load in loads:
        load.start()

    def wt_peer(d):
        return (b, lax.rem(w + d, n_wt))

    def seq_peer(d):
        return (lax.rem(b + d, n_seq), w)

    barrier = pltpu.get_barrier_semaphore()
    for d in range(1, n_wt):
        pl.semaphore_signal(barrier, inc=1, device_id=wt_peer(d), device_id_type=MESH)
    for d in range(1, n_seq):
        pl.semaphore_signal(barrier, inc=1, device_id=seq_peer(d), device_id_type=MESH)
    last_row = x_ref[shard - 1 : shard, :].astype(F32)
    for i in range(8):
        edge_src[i : i + 1, :] = last_row[:, i * piece : (i + 1) * piece]
    mine = pl.ds(pl.multiple_of(w * shard, shard), shard)
    x_all[mine, :] = x_ref[...]
    pl.semaphore_wait(barrier, n_wt + n_seq - 2)

    def remote(src, dst, send, recv, target):
        return pltpu.make_async_remote_copy(
            src_ref=src, dst_ref=dst, send_sem=send, recv_sem=recv, device_id=target, device_id_type=MESH
        )

    edge_copy = remote(edge_src, edge_in, edge_sem.at[0], edge_sem.at[1], seq_peer(1))
    forwards = [
        remote(edge_in, edge_in, fwd_sem.at[d - 1], edge_sem.at[1], wt_peer(d)) for d in range(1, n_wt)
    ]
    is_last = w == n_wt - 1

    @pl.when(is_last)
    def _():
        edge_copy.start()

    half = shard // 2

    def line_copy(step, part_no, up):
        owner = w - step if up else w + step
        place = x_all.at[pl.ds(pl.multiple_of(owner * shard + part_no * half, half), half)]
        side = 0 if up else 1
        return remote(
            place, place, x_send.at[side, step, part_no], x_recv.at[side, step, part_no],
            (b, w + 1 if up else w - 1),
        )

    def sends(step, up):
        return jnp.logical_and(w >= step, w + 1 < n_wt) if up else jnp.logical_and(w + step < n_wt, w >= 1)

    def gets(step, up):
        return w - 1 - step >= 0 if up else w + 1 + step < n_wt

    def line_step(step, part_no, up):
        if step > 0:
            @pl.when(gets(step - 1, up))
            def _():
                line_copy(step - 1, part_no, up).wait_recv()

        if step < n_wt - 1:
            @pl.when(sends(step, up))
            def _():
                line_copy(step, part_no, up).start()

    for part_no in range(2):
        for up in (True, False):
            line_step(0, part_no, up)
    edge_copy.wait_recv()

    @pl.when(is_last)
    def _():
        for copy in forwards:
            copy.start()
        edge_copy.wait_send()
        for copy in forwards:
            copy.wait_send()

    for step in range(1, n_wt):
        for part_no in range(2):
            for up in (True, False):
                line_step(step, part_no, up)
    for load in loads[:3]:
        load.wait()

    lengths = [len_ref[i] for i in range(len_ref.shape[0])]
    reset, seg_c, seg_r, seg_last = token_tables(b * rows, rows, lengths)
    edge = jnp.concatenate([edge_in[i : i + 1, :] for i in range(8)], axis=1)
    first_row = lax.broadcasted_iota(jnp.int32, (rows, 1), 0) == 0
    sums = [None] * 5
    step = min(512, model)
    for k in range(0, model, step):
        cols = slice(k, k + step)
        current = x_all[:, cols].astype(F32)
        previous = jnp.where(first_row, edge[:, cols], pltpu.roll(current, 1, 0))
        previous = jnp.where(reset == 1, 0.0, previous)
        delta = previous - current
        for c in range(5):
            mixed = (current + delta * rates_ref[c : c + 1, cols]).astype(BF16)
            if c < 3:
                term = mm(mixed, win[c, cols, :])
            else:
                term = mm(mixed, (d1_ref if c == 3 else a1_ref)[:, cols], 1, 1)
            sums[c] = term if sums[c] is None else sums[c] + term
    recept, keys, values = sums[:3]
    decay_in = jnp.dot(jnp.tanh(sums[3]).astype(BF16), d2_ref[...], preferred_element_type=F32)
    rate_in = jnp.dot(sums[4].astype(BF16), a2_ref[...], preferred_element_type=F32)
    chan = [ref[...] for ref in (db_ref, rb_ref, ks_ref, sh_ref, co_ref, ga_ref)]
    maps, adds, pending, keys_mod = block_terms(
        recept, keys, values, decay_in, rate_in, chan, seg_c, seg_r, seg_last
    )
    for h in range(heads):
        lo_src[0, :, head_slice(h)] = maps[h].astype(STATE_TYPE)
        lo_src[1, :, head_slice(h)] = adds[h].astype(STATE_TYPE)
    pair_copy = remote(lo_src, pair_in, pair_sem.at[0], pair_sem.at[1], (b + 1 - 2 * odd, w))
    pair_copy.start()
    reads, offsets = read_terms(pending)
    pair_copy.wait_recv()
    is_odd = odd == 1
    mine_lo = lo_src[...].astype(F32)
    other_lo = pair_in[...].astype(F32)
    even_lo = jnp.where(is_odd, other_lo, mine_lo)
    odd_lo = jnp.where(is_odd, mine_lo, other_lo)
    for h in range(heads):
        s = head_slice(h)
        both = mm(odd_lo[0, :, s], jnp.concatenate([even_lo[0, :, s], even_lo[1, :, s]], axis=1))
        chip_src[0, :, s] = both[:, :HS].astype(STATE_TYPE)
        chip_src[1, :, s] = (both[:, HS:] + odd_lo[1, :, s]).astype(STATE_TYPE)
    lo_copies = [
        remote(chip_src, lo_in.at[d - 1], lo_send.at[d - 1], lo_recv.at[d - 1], seq_peer(2 * d))
        for d in range(1, hops)
    ]
    lo_copies.append(
        remote(
            chip_src.at[1], lo_in.at[hops - 1, 1], lo_send.at[hops - 1], lo_recv.at[hops - 1],
            seq_peer(2 * hops),
        )
    )
    for copy in lo_copies:
        copy.start()
    for copy in lo_copies:
        copy.wait_recv()
    lo_copies.append(pair_copy)
    state = [lo_in[hops - 1, 1, :, head_slice(h)].astype(F32) for h in range(heads)]
    for d in range(hops - 2, -1, -1):
        state = [
            mm(lo_in[d, 0, :, head_slice(h)], state[h]) + lo_in[d, 1, :, head_slice(h)].astype(F32)
            for h in range(heads)
        ]
    state = [
        jnp.where(
            is_odd,
            mm(even_lo[0, :, head_slice(h)], state[h]) + even_lo[1, :, head_slice(h)],
            state[h],
        )
        for h in range(heads)
    ]
    heads_y = [mm(reads[h], state[h]) + offsets[h] for h in range(heads)]
    head_mix = finish_heads(heads_y, recept, keys_mod, values, chan[4], chan[5])

    loads[3].wait()
    for k in range(0, model, step):
        cols = slice(k, k + step)
        term = jnp.dot(head_mix, wout[:, cols], preferred_element_type=F32)
        part[:, cols] = term
    def owner_rows(owner, part_no):
        return pl.ds(pl.multiple_of(owner * shard + part_no * half, half), half)

    def sum_copy(step, part_no, up):
        owner = n_wt - 1 - step if up else step
        side = 0 if up else 1
        return remote(
            rs_src.at[side, step, part_no], rs_in.at[side, step, part_no],
            rs_send.at[side, step, part_no], rs_recv.at[side, step, part_no],
            (b, w + 1 if up else w - 1),
        ), owner

    def on_way(owner, up):
        return w < owner if up else w > owner

    for step in range(n_wt - 1):
        for part_no in range(2):
            for up in (True, False):
                copy, owner = sum_copy(step, part_no, up)
                side = 0 if up else 1
                inner = (w > 0) if up else (w < n_wt - 1)
                own = slice(owner * shard + part_no * half, owner * shard + (part_no + 1) * half)

                @pl.when(on_way(owner, up))
                def _():
                    @pl.when(inner)
                    def _():
                        copy.wait_recv()
                        rs_src[side, step, part_no] = (
                            part[own, :] + rs_in[side, step, part_no].astype(F32)
                        ).astype(BF16)

                    @pl.when(jnp.logical_not(inner))
                    def _():
                        rs_src[side, step, part_no] = part[own, :].astype(BF16)

                    copy.start()

    for part_no in range(2):
        here = slice(part_no * half, (part_no + 1) * half)
        out_ref_rows = owner_rows(w, part_no)
        acc[here, :] = part[out_ref_rows, :] + x_ref[here, :].astype(F32)
        for step in range(n_wt):
            for up in (True, False):
                if step < n_wt - 1:
                    copy, owner = sum_copy(step, part_no, up)
                    side = 0 if up else 1
                    inner = (w > 0) if up else (w < n_wt - 1)

                    @pl.when(jnp.logical_and(w == owner, inner))
                    def _():
                        copy.wait_recv()
                        acc[here, :] += rs_in[side, step, part_no].astype(F32)
    out_ref[...] = acc[...].astype(out_ref.dtype)
    for copy in lo_copies:
        copy.wait_send()
    for step in range(n_wt - 1):
        for part_no in range(2):
            for up in (True, False):
                copy, owner = sum_copy(step, part_no, up)

                @pl.when(sends(step, up))
                def _():
                    line_copy(step, part_no, up).wait_send()

                @pl.when(on_way(owner, up))
                def _():
                    copy.wait_send()


def shards(
    n_seq, n_wt,
    layer_input, token_shift_rates, input_projection_weight, output_matrix,
    decay_lowrank_first, decay_lowrank_second, learning_rate_first, learning_rate_second,
    decay_channel_bias, learning_rate_bias, prenorm_key_scale, written_key_share,
    present_step_coefficient, head_norm_gain, packed_request_length,
):
    shard, model = layer_input.shape
    rows = shard * n_wt
    width = decay_lowrank_second.shape[1]
    hops = (n_seq // 2 + 1) // 2
    chan = [
        v.reshape(1, width)
        for v in (
            decay_channel_bias, learning_rate_bias, prenorm_key_scale,
            written_key_share, present_step_coefficient, head_norm_gain,
        )
    ]
    vmem = pl.BlockSpec(memory_space=pltpu.VMEM)
    far = pl.BlockSpec(memory_space=pl.ANY)
    dma = pltpu.SemaphoreType.DMA
    return pl.pallas_call(
        functools.partial(kernel, n_seq, n_wt, hops),
        out_shape=jax.ShapeDtypeStruct((shard, model), BF16),
        in_specs=[vmem, vmem, far, far] + [vmem] * 10 + [pl.BlockSpec(memory_space=pltpu.SMEM)],
        out_specs=vmem,
        scratch_shapes=[
            pltpu.VMEM((rows, model), BF16),
            pltpu.VMEM((8, model // 8), F32),
            pltpu.VMEM((8, model // 8), F32),
            pltpu.VMEM((3, model, width), BF16),
            pltpu.VMEM((width, model), BF16),
            pltpu.VMEM((2, HS, width), STATE_TYPE),
            pltpu.VMEM((hops, 2, HS, width), STATE_TYPE),
            pltpu.VMEM((rows, model), F32),
            pltpu.VMEM((shard, model), F32),
            pltpu.VMEM((2, n_wt - 1, 2, shard // 2, model), BF16),
            pltpu.VMEM((2, n_wt - 1, 2, shard // 2, model), BF16),
            pltpu.VMEM((2, HS, width), STATE_TYPE),
            pltpu.VMEM((2, HS, width), STATE_TYPE),
            dma((4,)), dma((2,)), dma((2,)), dma((n_wt - 1,)),
            dma((2, n_wt - 1, 2)), dma((2, n_wt - 1, 2)),
            dma((hops,)), dma((hops,)),
            dma((2, n_wt - 1, 2)), dma((2, n_wt - 1, 2)),
        ],
        compiler_params=pltpu.CompilerParams(
            collective_id=0, has_side_effects=True, vmem_limit_bytes=56 * 1024 * 1024
        ),
    )(
        layer_input, token_shift_rates, input_projection_weight, output_matrix,
        decay_lowrank_first.T, decay_lowrank_second, learning_rate_first.T, learning_rate_second,
        *chan, packed_request_length,
    )


def solution(mesh):
    placed = (
        P(("seq", "wt"), None),
        P(),
        P(None, None, "wt"),
        P("wt", None),
        P(),
        P(None, "wt"),
        P(),
        P(None, "wt"),
        P("wt"),
        P("wt"),
        P("wt"),
        P("wt"),
        P("wt"),
        P("wt"),
        P(),
    )
    return jax.shard_map(
        functools.partial(shards, mesh.shape["seq"], mesh.shape["wt"]),
        mesh=mesh, in_specs=placed, out_specs=P(("seq", "wt"), None), check_vma=False,
    )
```

```python
import functools
import jax
import jax.numpy as jnp
from jax import lax
from jax.experimental import pallas as pl
from jax.experimental.pallas import tpu as pltpu
from jax.sharding import PartitionSpec as P

HS = 64
LOG_SCALE = 0.6065306597126334
MESH = pl.DeviceIdType.MESH
F32 = jnp.float32
BF16 = jnp.bfloat16
STATE_TYPE = BF16


def mm(a, b, ca=1, cb=0):
    return lax.dot_general(
        a.astype(BF16), b.astype(BF16), (((ca,), (cb,)), ((), ())), preferred_element_type=F32
    )


def mm_full(a, b, ca=1, cb=0):
    return lax.dot_general(
        a, b, (((ca,), (cb,)), ((), ())), preferred_element_type=F32, precision=lax.Precision.HIGHEST
    )


def token_tables(first, rows, lengths):
    pos_c = first + lax.broadcasted_iota(jnp.int32, (rows, 1), 0)
    pos_r = first + lax.broadcasted_iota(jnp.int32, (1, rows), 1)
    far = jnp.int32(2**30)
    start = jnp.int32(0)
    reset = jnp.zeros((rows, 1), jnp.int32)
    seg_c = jnp.zeros((rows, 1), jnp.int32)
    seg_r = jnp.zeros((1, rows), jnp.int32)
    seg_last = jnp.int32(0)
    for length in lengths:
        reset = jnp.maximum(reset, jnp.where(pos_c == start, 1, 0))
        inside = jnp.where(start >= first, start, far)
        seg_c = seg_c + jnp.where(pos_c >= inside, 1, 0)
        seg_r = seg_r + jnp.where(pos_r >= inside, 1, 0)
        seg_last = seg_last + jnp.where(first + (rows - 1) >= inside, 1, 0)
        start = start + length
    return reset, seg_c, seg_r, seg_last


def head_slice(h):
    return slice(h * HS, (h + 1) * HS)


def per_head(fn, width):
    return jnp.concatenate([fn(head_slice(h)) for h in range(width // HS)], axis=1)


def block_terms(recept, keys, values, decay_in, rate_in, chan, seg_c, seg_r, seg_last):
    rows, width = keys.shape
    heads = width // HS
    decay_bias, rate_bias, key_scale, share = chan[:4]
    logw = -LOG_SCALE * jax.nn.sigmoid(decay_bias + decay_in)
    rate = jax.nn.sigmoid(rate_bias + rate_in)
    row = lax.broadcasted_iota(jnp.int32, (rows, rows), 0)
    col = lax.broadcasted_iota(jnp.int32, (rows, rows), 1)
    tri = jnp.where(row >= col, 1.0, 0.0).astype(F32)
    cum = mm_full(tri, logw)
    center = cum[rows // 2 - 1 : rows // 2]
    last = cum[rows - 1 : rows]
    grow = jnp.exp(cum - center)
    grow_x = jnp.exp(cum - logw - center)
    shrink = jnp.exp(center - cum)
    to_start = jnp.exp(center) * jnp.where(seg_c == 0, 1.0, 0.0)
    to_end = jnp.exp(last - center) * jnp.where(seg_c == seg_last, 1.0, 0.0)
    scaled = keys * key_scale
    squares = scaled * scaled
    norm = per_head(
        lambda s: jnp.broadcast_to(
            lax.rsqrt(jnp.sum(squares[:, s], axis=1, keepdims=True) + 1e-06), (rows, HS)
        ),
        width,
    )
    unit = scaled * norm
    keys_mod = keys * (1.0 + (rate - 1.0) * share)
    u_c = unit * grow_x
    q_c = recept * grow
    r_c = unit * rate * shrink
    k_c = keys_mod * shrink
    u_0 = u_c * to_start
    q_0 = q_c * to_start
    r_e = r_c * to_end
    k_e = k_c * to_end
    same = seg_c == seg_r
    strict = jnp.logical_and(same, row > col)
    causal = jnp.logical_and(same, row >= col)
    a_ur, a_uk, a_qr, a_qk = [], [], [], []
    for h in range(heads):
        s = head_slice(h)
        left = jnp.concatenate([u_c[:, s], q_c[:, s]], axis=0)
        right = jnp.concatenate([r_c[:, s], k_c[:, s]], axis=0)
        pair = mm(left, right, 1, 1)
        a_ur.append(jnp.where(strict, pair[:rows, :rows], 0.0))
        a_uk.append(jnp.where(strict, pair[:rows, rows:], 0.0).astype(BF16))
        a_qr.append(jnp.where(causal, pair[rows:, :rows], 0.0).astype(BF16))
        a_qk.append(jnp.where(causal, pair[rows:, rows:], 0.0).astype(BF16))
    eye = jnp.where(row == col, 1.0, 0.0)
    inverse = None
    size = 1
    while size < rows:
        tile_r, tile_c = row // size, col // size
        corner = jnp.logical_and(tile_r == tile_c + 1, tile_r % 2 == 1)
        lows = [jnp.where(corner, a, 0.0) for a in a_ur]
        if inverse is None:
            inverse = [eye - low for low in lows]
        else:
            halves = [mm(x, low) for x, low in zip(inverse, lows)]
            inverse = [x - mm(half, x) for x, half in zip(inverse, halves)]
        size *= 2
    small_r = lax.broadcasted_iota(jnp.int32, (HS, HS), 0)
    small_c = lax.broadcasted_iota(jnp.int32, (HS, HS), 1)
    decay_all = jnp.exp(last) * jnp.where(seg_last == 0, 1.0, 0.0)
    maps, adds, pending = [], [], []
    for h in range(heads):
        s = head_slice(h)
        v = values[:, s].astype(BF16)
        kv = mm(jnp.concatenate([a_uk[h], a_qk[h]], axis=0), v)
        solved = mm(inverse[h], jnp.concatenate([u_0[:, s], kv[:rows]], axis=1)).astype(BF16)
        end = mm(r_e[:, s], solved, 0, 0)
        diag = jnp.where(small_r == small_c, jnp.broadcast_to(decay_all[:, s], (HS, HS)), 0.0)
        maps.append(diag - end[:, :HS])
        adds.append(mm(k_e[:, s], v, 0, 0) - end[:, HS:])
        pending.append((a_qr[h], solved, q_0[:, s], kv[rows:]))
    return maps, adds, pending, keys_mod


def read_terms(pending):
    reads, offsets = [], []
    for a_qr, solved, q_0, direct in pending:
        out = jnp.concatenate([q_0, direct], axis=1) - mm(a_qr, solved)
        reads.append(out[:, :HS].astype(BF16))
        offsets.append(out[:, HS:])
    return reads, offsets


def finish_heads(heads_y, recept, keys_mod, values, coefficient, gain):
    own = recept * keys_mod * coefficient
    mixed = []
    for h, y in enumerate(heads_y):
        s = head_slice(h)
        centered = y - jnp.mean(y, axis=1, keepdims=True)
        spread = jnp.mean(centered * centered, axis=1, keepdims=True)
        normed = centered * lax.rsqrt(spread + 0.00064) * gain[:, s]
        mixed.append(normed + jnp.sum(own[:, s], axis=1, keepdims=True) * values[:, s])
    return jnp.concatenate(mixed, axis=1).astype(BF16)


def kernel(
    n_seq, n_wt, hops,
    x_ref, rates_ref, win_hbm, wout_hbm, d1_ref, d2_ref, a1_ref, a2_ref,
    db_ref, rb_ref, ks_ref, sh_ref, co_ref, ga_ref, len_ref,
    out_ref,
    x_all, edge_src, edge_in, win, wout, lo_src, lo_in, part, part_16, rs_in, pair_in, chip_src,
    w_sem, pair_sem, edge_sem, fwd_sem, x_send, x_recv, lo_send, lo_recv, rs_send, rs_recv,
):
    b = lax.axis_index("seq")
    w = lax.axis_index("wt")
    shard, model = x_ref.shape
    rows = shard * n_wt
    width = win.shape[2]
    heads = width // HS
    odd = lax.rem(b, 2)
    piece = model // 8

    loads = [pltpu.make_async_copy(win_hbm.at[c], win.at[c], w_sem.at[c]) for c in range(3)]
    loads.append(pltpu.make_async_copy(wout_hbm, wout, w_sem.at[3]))
    for load in loads:
        load.start()

    def wt_peer(d):
        return (b, lax.rem(w + d, n_wt))

    def seq_peer(d):
        return (lax.rem(b + d, n_seq), w)

    barrier = pltpu.get_barrier_semaphore()
    for d in range(1, n_wt):
        pl.semaphore_signal(barrier, inc=1, device_id=wt_peer(d), device_id_type=MESH)
    for d in range(1, n_seq):
        pl.semaphore_signal(barrier, inc=1, device_id=seq_peer(d), device_id_type=MESH)
    last_row = x_ref[shard - 1 : shard, :].astype(F32)
    for i in range(8):
        edge_src[i : i + 1, :] = last_row[:, i * piece : (i + 1) * piece]
    mine = pl.ds(pl.multiple_of(w * shard, shard), shard)
    x_all[mine, :] = x_ref[...]
    pl.semaphore_wait(barrier, n_wt + n_seq - 2)

    def remote(src, dst, send, recv, target):
        return pltpu.make_async_remote_copy(
            src_ref=src, dst_ref=dst, send_sem=send, recv_sem=recv, device_id=target, device_id_type=MESH
        )

    edge_copy = remote(edge_src, edge_in, edge_sem.at[0], edge_sem.at[1], seq_peer(1))
    forwards = [
        remote(edge_in, edge_in, fwd_sem.at[d - 1], edge_sem.at[1], wt_peer(d)) for d in range(1, n_wt)
    ]
    is_last = w == n_wt - 1

    @pl.when(is_last)
    def _():
        edge_copy.start()

    x_copies = [
        remote(x_ref, x_all.at[mine], x_send.at[d - 1], x_recv.at[d - 1], wt_peer(d))
        for d in range(1, n_wt)
    ]
    top = n_wt - 1
    relayed = [d for d in (2, n_wt - 2)] if n_wt > 3 else []
    order = sorted(range(1, n_wt), key=lambda d: (d not in relayed, d))

    def direct(d):
        if not relayed or d not in (1, top):
            return w >= 0
        return w != (top if d == 1 else 0)

    def relay_copy(owner, target, d):
        place = x_all.at[pl.ds(owner * shard, shard)]
        return remote(place, place, fwd_sem.at[n_wt - 1], x_recv.at[d - 1], (b, target))

    relays = [(n_wt - 2, 0, top, top), (1, top, 0, 1)] if relayed else []
    for d in order:
        @pl.when(direct(d))
        def _():
            x_copies[d - 1].start()

    @pl.when(is_last)
    def _():
        edge_copy.wait_recv()
        for copy in forwards:
            copy.start()

    for d in sorted(set(relayed)):
        x_copies[d - 1].wait_recv()
    for at, owner, target, d in relays:
        @pl.when(w == at)
        def _():
            relay_copy(owner, target, d).start()

    @pl.when(w != top)
    def _():
        edge_copy.wait_recv()

    for d in range(1, n_wt):
        if d not in relayed:
            x_copies[d - 1].wait_recv()
    for load in loads[:3]:
        load.wait()

    lengths = [len_ref[i] for i in range(len_ref.shape[0])]
    reset, seg_c, seg_r, seg_last = token_tables(b * rows, rows, lengths)
    edge = jnp.concatenate([edge_in[i : i + 1, :] for i in range(8)], axis=1)
    first_row = lax.broadcasted_iota(jnp.int32, (rows, 1), 0) == 0
    sums = [None] * 5
    step = min(512, model)
    for k in range(0, model, step):
        cols = slice(k, k + step)
        current = x_all[:, cols].astype(F32)
        previous = jnp.where(first_row, edge[:, cols], pltpu.roll(current, 1, 0))
        previous = jnp.where(reset == 1, 0.0, previous)
        delta = previous - current
        for c in range(5):
            mixed = (current + delta * rates_ref[c : c + 1, cols]).astype(BF16)
            if c < 3:
                term = mm(mixed, win[c, cols, :])
            else:
                term = mm(mixed, (d1_ref if c == 3 else a1_ref)[:, cols], 1, 1)
            sums[c] = term if sums[c] is None else sums[c] + term
    recept, keys, values = sums[:3]
    decay_in = jnp.dot(jnp.tanh(sums[3]).astype(BF16), d2_ref[...], preferred_element_type=F32)
    rate_in = jnp.dot(sums[4].astype(BF16), a2_ref[...], preferred_element_type=F32)
    chan = [ref[...] for ref in (db_ref, rb_ref, ks_ref, sh_ref, co_ref, ga_ref)]
    maps, adds, pending, keys_mod = block_terms(
        recept, keys, values, decay_in, rate_in, chan, seg_c, seg_r, seg_last
    )
    for h in range(heads):
        lo_src[0, :, head_slice(h)] = maps[h].astype(STATE_TYPE)
        lo_src[1, :, head_slice(h)] = adds[h].astype(STATE_TYPE)
    pair_copy = remote(lo_src, pair_in, pair_sem.at[0], pair_sem.at[1], (b + 1 - 2 * odd, w))
    pair_copy.start()
    reads, offsets = read_terms(pending)
    pair_copy.wait_recv()
    is_odd = odd == 1
    mine_lo = lo_src[...].astype(F32)
    other_lo = pair_in[...].astype(F32)
    even_lo = jnp.where(is_odd, other_lo, mine_lo)
    odd_lo = jnp.where(is_odd, mine_lo, other_lo)
    for h in range(heads):
        s = head_slice(h)
        both = mm(odd_lo[0, :, s], jnp.concatenate([even_lo[0, :, s], even_lo[1, :, s]], axis=1))
        chip_src[0, :, s] = both[:, :HS].astype(STATE_TYPE)
        chip_src[1, :, s] = (both[:, HS:] + odd_lo[1, :, s]).astype(STATE_TYPE)
    lo_copies = [
        remote(chip_src, lo_in.at[d - 1], lo_send.at[d - 1], lo_recv.at[d - 1], seq_peer(2 * d))
        for d in range(1, hops)
    ]
    lo_copies.append(
        remote(
            chip_src.at[1], lo_in.at[hops - 1, 1], lo_send.at[hops - 1], lo_recv.at[hops - 1],
            seq_peer(2 * hops),
        )
    )
    for copy in lo_copies:
        copy.start()
    for copy in lo_copies:
        copy.wait_recv()
    lo_copies.append(pair_copy)
    state = [lo_in[hops - 1, 1, :, head_slice(h)].astype(F32) for h in range(heads)]
    for d in range(hops - 2, -1, -1):
        state = [
            mm(lo_in[d, 0, :, head_slice(h)], state[h]) + lo_in[d, 1, :, head_slice(h)].astype(F32)
            for h in range(heads)
        ]
    state = [
        jnp.where(
            is_odd,
            mm(even_lo[0, :, head_slice(h)], state[h]) + even_lo[1, :, head_slice(h)],
            state[h],
        )
        for h in range(heads)
    ]
    heads_y = [mm(reads[h], state[h]) + offsets[h] for h in range(heads)]
    head_mix = finish_heads(heads_y, recept, keys_mod, values, chan[4], chan[5])

    loads[3].wait()
    for k in range(0, model, step):
        cols = slice(k, k + step)
        term = jnp.dot(head_mix, wout[:, cols], preferred_element_type=F32)
        part[:, cols] = term
        part_16[:, cols] = term.astype(BF16)
    rs_copies = []
    for d in range(1, n_wt):
        there = pl.ds(pl.multiple_of(lax.rem(w + d, n_wt) * shard, shard), shard)
        rs_copies.append(
            remote(part_16.at[there], rs_in.at[d - 1], rs_send.at[d - 1], rs_recv.at[d - 1], wt_peer(d))
        )
    for copy in rs_copies:
        copy.start()
    total = part[mine, :] + x_ref[...].astype(F32)
    for d, copy in enumerate(rs_copies):
        copy.wait_recv()
        total = total + rs_in[d].astype(F32)
    out_ref[...] = total.astype(out_ref.dtype)
    for copy in lo_copies + rs_copies:
        copy.wait_send()
    for d in range(1, n_wt):
        @pl.when(direct(d))
        def _():
            x_copies[d - 1].wait_send()

    for at, owner, target, d in relays:
        @pl.when(w == at)
        def _():
            relay_copy(owner, target, d).wait_send()

    @pl.when(is_last)
    def _():
        edge_copy.wait_send()
        for copy in forwards:
            copy.wait_send()


def shards(
    n_seq, n_wt,
    layer_input, token_shift_rates, input_projection_weight, output_matrix,
    decay_lowrank_first, decay_lowrank_second, learning_rate_first, learning_rate_second,
    decay_channel_bias, learning_rate_bias, prenorm_key_scale, written_key_share,
    present_step_coefficient, head_norm_gain, packed_request_length,
):
    shard, model = layer_input.shape
    rows = shard * n_wt
    width = decay_lowrank_second.shape[1]
    hops = (n_seq // 2 + 1) // 2
    chan = [
        v.reshape(1, width)
        for v in (
            decay_channel_bias, learning_rate_bias, prenorm_key_scale,
            written_key_share, present_step_coefficient, head_norm_gain,
        )
    ]
    vmem = pl.BlockSpec(memory_space=pltpu.VMEM)
    far = pl.BlockSpec(memory_space=pl.ANY)
    dma = pltpu.SemaphoreType.DMA
    return pl.pallas_call(
        functools.partial(kernel, n_seq, n_wt, hops),
        out_shape=jax.ShapeDtypeStruct((shard, model), BF16),
        in_specs=[vmem, vmem, far, far] + [vmem] * 10 + [pl.BlockSpec(memory_space=pltpu.SMEM)],
        out_specs=vmem,
        scratch_shapes=[
            pltpu.VMEM((rows, model), BF16),
            pltpu.VMEM((8, model // 8), F32),
            pltpu.VMEM((8, model // 8), F32),
            pltpu.VMEM((3, model, width), BF16),
            pltpu.VMEM((width, model), BF16),
            pltpu.VMEM((2, HS, width), STATE_TYPE),
            pltpu.VMEM((hops, 2, HS, width), STATE_TYPE),
            pltpu.VMEM((rows, model), F32),
            pltpu.VMEM((rows, model), BF16),
            pltpu.VMEM((n_wt - 1, shard, model), BF16),
            pltpu.VMEM((2, HS, width), STATE_TYPE),
            pltpu.VMEM((2, HS, width), STATE_TYPE),
            dma((4,)), dma((2,)), dma((2,)), dma((n_wt,)),
            dma((n_wt - 1,)), dma((n_wt - 1,)),
            dma((hops,)), dma((hops,)),
            dma((n_wt - 1,)), dma((n_wt - 1,)),
        ],
        compiler_params=pltpu.CompilerParams(
            collective_id=0, has_side_effects=True, vmem_limit_bytes=56 * 1024 * 1024
        ),
    )(
        layer_input, token_shift_rates, input_projection_weight, output_matrix,
        decay_lowrank_first.T, decay_lowrank_second, learning_rate_first.T, learning_rate_second,
        *chan, packed_request_length,
    )


def solution(mesh):
    placed = (
        P(("seq", "wt"), None),
        P(),
        P(None, None, "wt"),
        P("wt", None),
        P(),
        P(None, "wt"),
        P(),
        P(None, "wt"),
        P("wt"),
        P("wt"),
        P("wt"),
        P("wt"),
        P("wt"),
        P("wt"),
        P(),
    )
    return jax.shard_map(
        functools.partial(shards, mesh.shape["seq"], mesh.shape["wt"]),
        mesh=mesh, in_specs=placed, out_specs=P(("seq", "wt"), None), check_vma=False,
    )
```

```python
import functools
import jax
import jax.numpy as jnp
from jax import lax
from jax.experimental import pallas as pl
from jax.experimental.pallas import tpu as pltpu
from jax.sharding import PartitionSpec as P

HS = 64
LOG_SCALE = 0.6065306597126334
MESH = pl.DeviceIdType.MESH
F32 = jnp.float32
BF16 = jnp.bfloat16
STATE_TYPE = BF16


def mm(a, b, ca=1, cb=0):
    return lax.dot_general(
        a.astype(BF16), b.astype(BF16), (((ca,), (cb,)), ((), ())), preferred_element_type=F32
    )


def mm_full(a, b, ca=1, cb=0):
    return lax.dot_general(
        a, b, (((ca,), (cb,)), ((), ())), preferred_element_type=F32, precision=lax.Precision.HIGHEST
    )


def token_tables(first, rows, lengths):
    pos_c = first + lax.broadcasted_iota(jnp.int32, (rows, 1), 0)
    pos_r = first + lax.broadcasted_iota(jnp.int32, (1, rows), 1)
    far = jnp.int32(2**30)
    start = jnp.int32(0)
    reset = jnp.zeros((rows, 1), jnp.int32)
    seg_c = jnp.zeros((rows, 1), jnp.int32)
    seg_r = jnp.zeros((1, rows), jnp.int32)
    seg_last = jnp.int32(0)
    for length in lengths:
        reset = jnp.maximum(reset, jnp.where(pos_c == start, 1, 0))
        inside = jnp.where(start >= first, start, far)
        seg_c = seg_c + jnp.where(pos_c >= inside, 1, 0)
        seg_r = seg_r + jnp.where(pos_r >= inside, 1, 0)
        seg_last = seg_last + jnp.where(first + (rows - 1) >= inside, 1, 0)
        start = start + length
    return reset, seg_c, seg_r, seg_last


def head_slice(h):
    return slice(h * HS, (h + 1) * HS)


def per_head(fn, width):
    return jnp.concatenate([fn(head_slice(h)) for h in range(width // HS)], axis=1)


def block_terms(recept, keys, values, decay_in, rate_in, chan, seg_c, seg_r, seg_last):
    rows, width = keys.shape
    heads = width // HS
    decay_bias, rate_bias, key_scale, share = chan[:4]
    logw = -LOG_SCALE * jax.nn.sigmoid(decay_bias + decay_in)
    rate = jax.nn.sigmoid(rate_bias + rate_in)
    row = lax.broadcasted_iota(jnp.int32, (rows, rows), 0)
    col = lax.broadcasted_iota(jnp.int32, (rows, rows), 1)
    tri = jnp.where(row >= col, 1.0, 0.0).astype(F32)
    cum = mm_full(tri, logw)
    center = cum[rows // 2 - 1 : rows // 2]
    last = cum[rows - 1 : rows]
    grow = jnp.exp(cum - center)
    grow_x = jnp.exp(cum - logw - center)
    shrink = jnp.exp(center - cum)
    to_start = jnp.exp(center) * jnp.where(seg_c == 0, 1.0, 0.0)
    to_end = jnp.exp(last - center) * jnp.where(seg_c == seg_last, 1.0, 0.0)
    scaled = keys * key_scale
    squares = scaled * scaled
    norm = per_head(
        lambda s: jnp.broadcast_to(
            lax.rsqrt(jnp.sum(squares[:, s], axis=1, keepdims=True) + 1e-06), (rows, HS)
        ),
        width,
    )
    unit = scaled * norm
    keys_mod = keys * (1.0 + (rate - 1.0) * share)
    u_c = unit * grow_x
    q_c = recept * grow
    r_c = unit * rate * shrink
    k_c = keys_mod * shrink
    u_0 = u_c * to_start
    q_0 = q_c * to_start
    r_e = r_c * to_end
    k_e = k_c * to_end
    same = seg_c == seg_r
    strict = jnp.logical_and(same, row > col)
    causal = jnp.logical_and(same, row >= col)
    a_ur, a_uk, a_qr, a_qk = [], [], [], []
    for h in range(heads):
        s = head_slice(h)
        left = jnp.concatenate([u_c[:, s], q_c[:, s]], axis=0)
        right = jnp.concatenate([r_c[:, s], k_c[:, s]], axis=0)
        pair = mm(left, right, 1, 1)
        a_ur.append(jnp.where(strict, pair[:rows, :rows], 0.0))
        a_uk.append(jnp.where(strict, pair[:rows, rows:], 0.0).astype(BF16))
        a_qr.append(jnp.where(causal, pair[rows:, :rows], 0.0).astype(BF16))
        a_qk.append(jnp.where(causal, pair[rows:, rows:], 0.0).astype(BF16))
    eye = jnp.where(row == col, 1.0, 0.0)
    inverse = None
    size = 1
    while size < rows:
        tile_r, tile_c = row // size, col // size
        corner = jnp.logical_and(tile_r == tile_c + 1, tile_r % 2 == 1)
        lows = [jnp.where(corner, a, 0.0) for a in a_ur]
        if inverse is None:
            inverse = [eye - low for low in lows]
        else:
            halves = [mm(x, low) for x, low in zip(inverse, lows)]
            inverse = [x - mm(half, x) for x, half in zip(inverse, halves)]
        size *= 2
    small_r = lax.broadcasted_iota(jnp.int32, (HS, HS), 0)
    small_c = lax.broadcasted_iota(jnp.int32, (HS, HS), 1)
    decay_all = jnp.exp(last) * jnp.where(seg_last == 0, 1.0, 0.0)
    maps, adds, pending = [], [], []
    for h in range(heads):
        s = head_slice(h)
        v = values[:, s].astype(BF16)
        kv = mm(jnp.concatenate([a_uk[h], a_qk[h]], axis=0), v)
        solved = mm(inverse[h], jnp.concatenate([u_0[:, s], kv[:rows]], axis=1)).astype(BF16)
        end = mm(r_e[:, s], solved, 0, 0)
        diag = jnp.where(small_r == small_c, jnp.broadcast_to(decay_all[:, s], (HS, HS)), 0.0)
        maps.append(diag - end[:, :HS])
        adds.append(mm(k_e[:, s], v, 0, 0) - end[:, HS:])
        pending.append((a_qr[h], solved, q_0[:, s], kv[rows:]))
    return maps, adds, pending, keys_mod


def read_terms(pending):
    reads, offsets = [], []
    for a_qr, solved, q_0, direct in pending:
        out = jnp.concatenate([q_0, direct], axis=1) - mm(a_qr, solved)
        reads.append(out[:, :HS].astype(BF16))
        offsets.append(out[:, HS:])
    return reads, offsets


def finish_heads(heads_y, recept, keys_mod, values, coefficient, gain):
    own = recept * keys_mod * coefficient
    mixed = []
    for h, y in enumerate(heads_y):
        s = head_slice(h)
        centered = y - jnp.mean(y, axis=1, keepdims=True)
        spread = jnp.mean(centered * centered, axis=1, keepdims=True)
        normed = centered * lax.rsqrt(spread + 0.00064) * gain[:, s]
        mixed.append(normed + jnp.sum(own[:, s], axis=1, keepdims=True) * values[:, s])
    return jnp.concatenate(mixed, axis=1).astype(BF16)


def kernel(
    n_seq, n_wt, hops,
    x_ref, rates_ref, win_hbm, wout_hbm, d1_ref, d2_ref, a1_ref, a2_ref,
    db_ref, rb_ref, ks_ref, sh_ref, co_ref, ga_ref, len_ref,
    out_ref,
    x_all, edge_src, edge_in, win, wout, lo_src, lo_in, part, part_16, rs_in, pair_in, chip_src, merge_in, acc,
    w_sem, merge_sem, pair_sem, edge_sem, fwd_sem, x_send, x_recv, lo_send, lo_recv, rs_send, rs_recv,
):
    b = lax.axis_index("seq")
    w = lax.axis_index("wt")
    shard, model = x_ref.shape
    rows = shard * n_wt
    width = win.shape[2]
    heads = width // HS
    odd = lax.rem(b, 2)
    piece = model // 8

    loads = [pltpu.make_async_copy(win_hbm.at[c], win.at[c], w_sem.at[c]) for c in range(3)]
    loads.append(pltpu.make_async_copy(wout_hbm, wout, w_sem.at[3]))
    for load in loads:
        load.start()

    def wt_peer(d):
        return (b, lax.rem(w + d, n_wt))

    def seq_peer(d):
        return (lax.rem(b + d, n_seq), w)

    barrier = pltpu.get_barrier_semaphore()
    for d in range(1, n_wt):
        pl.semaphore_signal(barrier, inc=1, device_id=wt_peer(d), device_id_type=MESH)
    for d in range(1, n_seq):
        pl.semaphore_signal(barrier, inc=1, device_id=seq_peer(d), device_id_type=MESH)
    last_row = x_ref[shard - 1 : shard, :].astype(F32)
    for i in range(8):
        edge_src[i : i + 1, :] = last_row[:, i * piece : (i + 1) * piece]
    mine = pl.ds(pl.multiple_of(w * shard, shard), shard)
    x_all[mine, :] = x_ref[...]
    pl.semaphore_wait(barrier, n_wt + n_seq - 2)

    def remote(src, dst, send, recv, target):
        return pltpu.make_async_remote_copy(
            src_ref=src, dst_ref=dst, send_sem=send, recv_sem=recv, device_id=target, device_id_type=MESH
        )

    edge_copy = remote(edge_src, edge_in, edge_sem.at[0], edge_sem.at[1], seq_peer(1))
    forwards = [
        remote(edge_in, edge_in, fwd_sem.at[d - 1], edge_sem.at[1], wt_peer(d)) for d in range(1, n_wt)
    ]
    is_last = w == n_wt - 1

    @pl.when(is_last)
    def _():
        edge_copy.start()

    x_copies = [
        remote(x_ref, x_all.at[mine], x_send.at[d - 1], x_recv.at[d - 1], wt_peer(d))
        for d in range(1, n_wt)
    ]
    top = n_wt - 1
    relayed = [d for d in (2, n_wt - 2)] if n_wt > 3 else []
    order = sorted(range(1, n_wt), key=lambda d: (d not in relayed, d))

    def direct(d):
        if not relayed or d not in (1, top):
            return w >= 0
        return w != (top if d == 1 else 0)

    def relay_copy(owner, target, d):
        place = x_all.at[pl.ds(owner * shard, shard)]
        return remote(place, place, fwd_sem.at[n_wt - 1], x_recv.at[d - 1], (b, target))

    relays = [(n_wt - 2, 0, top, top), (1, top, 0, 1)] if relayed else []
    for d in order:
        @pl.when(direct(d))
        def _():
            x_copies[d - 1].start()

    @pl.when(is_last)
    def _():
        edge_copy.wait_recv()
        for copy in forwards:
            copy.start()

    for d in sorted(set(relayed)):
        x_copies[d - 1].wait_recv()
    for at, owner, target, d in relays:
        @pl.when(w == at)
        def _():
            relay_copy(owner, target, d).start()

    @pl.when(w != top)
    def _():
        edge_copy.wait_recv()

    for d in range(1, n_wt):
        if d not in relayed:
            x_copies[d - 1].wait_recv()
    for load in loads[:3]:
        load.wait()

    lengths = [len_ref[i] for i in range(len_ref.shape[0])]
    reset, seg_c, seg_r, seg_last = token_tables(b * rows, rows, lengths)
    edge = jnp.concatenate([edge_in[i : i + 1, :] for i in range(8)], axis=1)
    first_row = lax.broadcasted_iota(jnp.int32, (rows, 1), 0) == 0
    sums = [None] * 5
    step = min(512, model)
    for k in range(0, model, step):
        cols = slice(k, k + step)
        current = x_all[:, cols].astype(F32)
        previous = jnp.where(first_row, edge[:, cols], pltpu.roll(current, 1, 0))
        previous = jnp.where(reset == 1, 0.0, previous)
        delta = previous - current
        for c in range(5):
            mixed = (current + delta * rates_ref[c : c + 1, cols]).astype(BF16)
            if c < 3:
                term = mm(mixed, win[c, cols, :])
            else:
                term = mm(mixed, (d1_ref if c == 3 else a1_ref)[:, cols], 1, 1)
            sums[c] = term if sums[c] is None else sums[c] + term
    recept, keys, values = sums[:3]
    decay_in = jnp.dot(jnp.tanh(sums[3]).astype(BF16), d2_ref[...], preferred_element_type=F32)
    rate_in = jnp.dot(sums[4].astype(BF16), a2_ref[...], preferred_element_type=F32)
    chan = [ref[...] for ref in (db_ref, rb_ref, ks_ref, sh_ref, co_ref, ga_ref)]
    maps, adds, pending, keys_mod = block_terms(
        recept, keys, values, decay_in, rate_in, chan, seg_c, seg_r, seg_last
    )
    for h in range(heads):
        lo_src[0, :, head_slice(h)] = maps[h].astype(STATE_TYPE)
        lo_src[1, :, head_slice(h)] = adds[h].astype(STATE_TYPE)
    pair_copy = remote(lo_src, pair_in, pair_sem.at[0], pair_sem.at[1], (b + 1 - 2 * odd, w))
    pair_copy.start()
    reads, offsets = read_terms(pending)
    pair_copy.wait_recv()
    is_odd = odd == 1
    mine_lo = lo_src[...].astype(F32)
    other_lo = pair_in[...].astype(F32)
    even_lo = jnp.where(is_odd, other_lo, mine_lo)
    odd_lo = jnp.where(is_odd, mine_lo, other_lo)
    for h in range(heads):
        s = head_slice(h)
        both = mm(odd_lo[0, :, s], jnp.concatenate([even_lo[0, :, s], even_lo[1, :, s]], axis=1))
        chip_src[0, :, s] = both[:, :HS].astype(STATE_TYPE)
        chip_src[1, :, s] = (both[:, HS:] + odd_lo[1, :, s]).astype(STATE_TYPE)
    lo_copies = [
        remote(chip_src, lo_in.at[d - 1], lo_send.at[d - 1], lo_recv.at[d - 1], seq_peer(2 * d))
        for d in range(1, hops)
    ]
    lo_copies.append(
        remote(
            chip_src.at[1], lo_in.at[hops - 1, 1], lo_send.at[hops - 1], lo_recv.at[hops - 1],
            seq_peer(2 * hops),
        )
    )
    for copy in lo_copies:
        copy.start()
    for copy in lo_copies:
        copy.wait_recv()
    lo_copies.append(pair_copy)
    state = [lo_in[hops - 1, 1, :, head_slice(h)].astype(F32) for h in range(heads)]
    for d in range(hops - 2, -1, -1):
        state = [
            mm(lo_in[d, 0, :, head_slice(h)], state[h]) + lo_in[d, 1, :, head_slice(h)].astype(F32)
            for h in range(heads)
        ]
    state = [
        jnp.where(
            is_odd,
            mm(even_lo[0, :, head_slice(h)], state[h]) + even_lo[1, :, head_slice(h)],
            state[h],
        )
        for h in range(heads)
    ]
    heads_y = [mm(reads[h], state[h]) + offsets[h] for h in range(heads)]
    head_mix = finish_heads(heads_y, recept, keys_mod, values, chan[4], chan[5])

    loads[3].wait()
    for k in range(0, model, step):
        cols = slice(k, k + step)
        term = jnp.dot(head_mix, wout[:, cols], preferred_element_type=F32)
        part[:, cols] = term
        part_16[:, cols] = term.astype(BF16)
    rs_copies = []
    for d in range(1, n_wt):
        there = pl.ds(pl.multiple_of(lax.rem(w + d, n_wt) * shard, shard), shard)
        rs_copies.append(
            remote(part_16.at[there], rs_in.at[d - 1], rs_send.at[d - 1], rs_recv.at[d - 1], wt_peer(d))
        )
    def end_rows(owner):
        return slice(owner * shard, (owner + 1) * shard)

    merges = [(0, 1, top, n_wt - 2), (top, top - 1, 0, 2)] if relayed else []

    def merge_copy(owner, target):
        return remote(part_16.at[pl.ds(owner * shard, shard)], merge_in, merge_sem.at[0], merge_sem.at[1], (b, target))

    def at_once(d):
        held = [jnp.logical_and(w == at, d == which) for _, at, _, which in merges if d == which]
        fine = direct(d)
        for one in held:
            fine = jnp.logical_and(fine, jnp.logical_not(one))
        return fine

    for end, at, owner, which in merges:
        @pl.when(w == end)
        def _():
            merge_copy(owner, at).start()

    for d in order:
        @pl.when(at_once(d))
        def _():
            rs_copies[d - 1].start()

    for end, at, owner, which in merges:
        @pl.when(w == at)
        def _():
            merge_copy(owner, at).wait_recv()
            part_16[end_rows(owner), :] = (
                part[end_rows(owner), :] + merge_in[...].astype(F32)
            ).astype(BF16)
            rs_copies[which - 1].start()

    acc[...] = part[mine, :] + x_ref[...].astype(F32)
    for d in sorted(range(1, n_wt), key=lambda d: (d in relayed, d)):
        absent = w == (0 if d == 1 else top) if relayed and d in (1, top) else w < 0

        @pl.when(jnp.logical_not(absent))
        def _():
            rs_copies[d - 1].wait_recv()
            acc[...] += rs_in[d - 1].astype(F32)

    total = acc[...]
    out_ref[...] = total.astype(out_ref.dtype)
    for copy in lo_copies:
        copy.wait_send()
    for d in range(1, n_wt):
        @pl.when(direct(d))
        def _():
            x_copies[d - 1].wait_send()
            rs_copies[d - 1].wait_send()

    for end, at, owner, which in merges:
        @pl.when(w == end)
        def _():
            merge_copy(owner, at).wait_send()

    for at, owner, target, d in relays:
        @pl.when(w == at)
        def _():
            relay_copy(owner, target, d).wait_send()

    @pl.when(is_last)
    def _():
        edge_copy.wait_send()
        for copy in forwards:
            copy.wait_send()


def shards(
    n_seq, n_wt,
    layer_input, token_shift_rates, input_projection_weight, output_matrix,
    decay_lowrank_first, decay_lowrank_second, learning_rate_first, learning_rate_second,
    decay_channel_bias, learning_rate_bias, prenorm_key_scale, written_key_share,
    present_step_coefficient, head_norm_gain, packed_request_length,
):
    shard, model = layer_input.shape
    rows = shard * n_wt
    width = decay_lowrank_second.shape[1]
    hops = (n_seq // 2 + 1) // 2
    chan = [
        v.reshape(1, width)
        for v in (
            decay_channel_bias, learning_rate_bias, prenorm_key_scale,
            written_key_share, present_step_coefficient, head_norm_gain,
        )
    ]
    vmem = pl.BlockSpec(memory_space=pltpu.VMEM)
    far = pl.BlockSpec(memory_space=pl.ANY)
    dma = pltpu.SemaphoreType.DMA
    return pl.pallas_call(
        functools.partial(kernel, n_seq, n_wt, hops),
        out_shape=jax.ShapeDtypeStruct((shard, model), BF16),
        in_specs=[vmem, vmem, far, far] + [vmem] * 10 + [pl.BlockSpec(memory_space=pltpu.SMEM)],
        out_specs=vmem,
        scratch_shapes=[
            pltpu.VMEM((rows, model), BF16),
            pltpu.VMEM((8, model // 8), F32),
            pltpu.VMEM((8, model // 8), F32),
            pltpu.VMEM((3, model, width), BF16),
            pltpu.VMEM((width, model), BF16),
            pltpu.VMEM((2, HS, width), STATE_TYPE),
            pltpu.VMEM((hops, 2, HS, width), STATE_TYPE),
            pltpu.VMEM((rows, model), F32),
            pltpu.VMEM((rows, model), BF16),
            pltpu.VMEM((n_wt - 1, shard, model), BF16),
            pltpu.VMEM((2, HS, width), STATE_TYPE),
            pltpu.VMEM((2, HS, width), STATE_TYPE),
            pltpu.VMEM((shard, model), BF16),
            pltpu.VMEM((shard, model), F32),
            dma((4,)), dma((2,)), dma((2,)), dma((2,)), dma((n_wt,)),
            dma((n_wt - 1,)), dma((n_wt - 1,)),
            dma((hops,)), dma((hops,)),
            dma((n_wt - 1,)), dma((n_wt - 1,)),
        ],
        compiler_params=pltpu.CompilerParams(
            collective_id=0, has_side_effects=True, vmem_limit_bytes=56 * 1024 * 1024
        ),
    )(
        layer_input, token_shift_rates, input_projection_weight, output_matrix,
        decay_lowrank_first.T, decay_lowrank_second, learning_rate_first.T, learning_rate_second,
        *chan, packed_request_length,
    )


def solution(mesh):
    placed = (
        P(("seq", "wt"), None),
        P(),
        P(None, None, "wt"),
        P("wt", None),
        P(),
        P(None, "wt"),
        P(),
        P(None, "wt"),
        P("wt"),
        P("wt"),
        P("wt"),
        P("wt"),
        P("wt"),
        P("wt"),
        P(),
    )
    return jax.shard_map(
        functools.partial(shards, mesh.shape["seq"], mesh.shape["wt"]),
        mesh=mesh, in_specs=placed, out_specs=P(("seq", "wt"), None), check_vma=False,
    )
```
